256 devices in a mesh: pts: 64 (over z, x, core), cen: 4 (over y).
Axes of the slice: x: 4, y: 4, z: 8, core: 2. Of those that a mesh axis runs over, the one named last changes fastest.
Arguments:
- points: bfloat16 [131072, 768], P('pts'), may hold values from -16 to 16
- centroids: bfloat16 [4096, 768], P('cen'), may hold values from -1 to 1
Outputs:
- new_centroids: bfloat16 [4096, 768], P(('cen', 'pts'))
- distances: float32 [131072], P('pts')
The draws below stay inside these ranges and needn't reach their ends.
All inputs are finite; a program needn't handle non-finite values.
Results may differ from the reference program's by a relative error of at most 0.0034.
Values may be sent and summed in bfloat16 or wider, within the bound.
No kernel may reach another device: no remote copies, remote signals or barrier semaphores. Data moves between devices by JAX's collectives and lax.ppermute only.
A program may use at most 64 MiB of HBM per device.

```python
import math
import jax
import jax.numpy as jnp
from jax import lax

D = 768
K = 4096
ITERS = 3
NPTS = 131072


def centroid_table(key):
    base = jax.random.fold_in(key, 7)
    table = jax.random.truncated_normal(base, -6.0, 6.0, (K, D), jnp.float32) * D ** (-0.5)
    return jnp.clip(table, -1.0, 1.0)


def draw_centroids(key, part):
    return centroid_table(key).astype(jnp.bfloat16)


def draw_points(key, part):
    base = jax.random.fold_in(key, 11)
    values = jax.random.truncated_normal(base, -6.0, 6.0, (NPTS, D), jnp.float32)
    return jnp.clip(values, -16.0, 16.0).astype(jnp.bfloat16)


def setup_inputs(seed: int = 0) -> dict:
    key_of = jax.random.split(jax.random.key(seed), 3)
    points = draw_points(jax.random.fold_in(key_of[2], 71), 0)
    centroids = draw_centroids(jax.random.fold_in(key_of[2], 71), 0)
    return dict(points=points, centroids=centroids)


sharpness = 4.0


def reference(points, centroids):
    scores = sharpness * jnp.dot(points, centroids.T, preferred_element_type=jnp.float32)
    col_potential = jnp.zeros((K,), jnp.float32)
    row_potential = jnp.zeros((NPTS,), jnp.float32)
    for iteration in range(ITERS):
        row_potential = -math.log(NPTS) - jax.nn.logsumexp(scores + col_potential[None, :], axis=1)
        col_potential = -math.log(K) - jax.nn.logsumexp(scores + row_potential[:, None], axis=0)
    blocksize = min(4096, NPTS)
    nblocks = NPTS // blocksize
    score_blocks = scores.reshape(nblocks, blocksize, K)
    potential_blocks = row_potential.reshape(nblocks, blocksize)
    point_blocks = points.reshape(nblocks, blocksize, D)

    def accumulate(carry, inputs):
        block_scores, block_rows, block_points = inputs
        transport = jnp.exp(block_scores + block_rows[:, None] + col_potential[None, :])
        weights = transport.astype(jnp.bfloat16)
        return carry + jnp.dot(weights.T, block_points, preferred_element_type=jnp.float32), None

    sums, unused = lax.scan(accumulate, jnp.zeros((K, D), jnp.float32), (score_blocks, potential_blocks, point_blocks))
    new_centroids = (K * sums).astype(jnp.bfloat16)
    squares = jnp.sum(new_centroids.astype(jnp.float32) ** 2, axis=1)

    def measure(inputs):
        block_scores, block_rows, block_points = inputs
        transport = jnp.exp(block_scores + block_rows[:, None] + col_potential[None, :])
        cross_terms = jnp.dot(block_points, new_centroids.T, preferred_element_type=jnp.float32)
        numerator = jnp.sum(transport * (squares[None, :] - 2.0 * cross_terms), axis=1)
        row_mass = jnp.sum(transport, axis=1)
        return numerator / row_mass / D

    distances = lax.map(measure, (score_blocks, potential_blocks, point_blocks)).reshape(NPTS)
    return new_centroids, distances
```

```python
import math

import jax
import jax.numpy as jnp
from jax import lax
from jax.sharding import PartitionSpec as P

ITERS = 3


sharpness = 4.0
LOG2E = math.log2(math.e)
C = 2


def other_core(value):
    size = lax.axis_size("pts")
    return lax.ppermute(value, "pts", [(i, i ^ 1) for i in range(size)])


def chip_groups():
    size = lax.axis_size("pts")
    return [[chip * C + core for chip in range(size // C)] for core in range(C)]


def exchange(value):
    return lax.all_to_all(value, "pts", 0, 0, axis_index_groups=chip_groups())


def from_chips(value):
    chips = lax.axis_size("pts") // C
    return exchange(jnp.broadcast_to(value[None], (chips,) + value.shape))


def cen_shift(value, step):
    size = lax.axis_size("cen")
    return lax.ppermute(value, "cen", [(i, (i + step) % size) for i in range(size)])


def merged_rows(value):
    one, two, three = [cen_shift(value, step) for step in (1, 2, 3)]
    top = jnp.maximum(jnp.maximum(value, two), jnp.maximum(one, three))
    even = jnp.exp2(value - top) + jnp.exp2(two - top)
    odd = jnp.exp2(one - top) + jnp.exp2(three - top)
    return top + jnp.log2(even + odd)


def merged_cols(value):
    theirs = other_core(value)
    top = jnp.maximum(value, theirs)
    value = top + jnp.log2(jnp.exp2(value - top) + jnp.exp2(theirs - top))
    values = from_chips(value)
    top = jnp.max(values, axis=0)
    return top + jnp.log2(jnp.sum(jnp.exp2(values - top[None]), axis=0))


def scattered(partial):
    core = lax.axis_index("pts") % C
    chips = lax.axis_size("pts") // C
    rows, width = partial.shape
    parts = partial.reshape(chips, C, rows // (chips * C), width)
    keep = lax.dynamic_index_in_dim(parts, core, 1, keepdims=False)
    give = lax.dynamic_index_in_dim(parts, 1 - core, 1, keepdims=False)
    theirs = other_core(give.astype(jnp.bfloat16)).astype(jnp.float32)
    pieces = exchange((keep + theirs).astype(jnp.bfloat16))
    return jnp.sum(pieces.astype(jnp.float32), axis=0)


def collected(own):
    core = lax.axis_index("pts") % C
    mine = from_chips(own)
    theirs = other_core(mine)
    first = jnp.where(core == 0, mine, theirs)
    second = jnp.where(core == 0, theirs, mine)
    return jnp.stack([first, second], axis=1).reshape(-1, own.shape[-1])


def on_device(points, centroids):
    total_points = points.shape[0] * lax.axis_size("pts")
    total_centroids = centroids.shape[0] * lax.axis_size("cen")
    width = points.shape[1]
    scores = (sharpness * LOG2E) * lax.dot_general(
        points, centroids, (((1,), (1,)), ((), ())), preferred_element_type=jnp.float32
    )
    col_potential = jnp.zeros((centroids.shape[0],), jnp.float32)
    for iteration in range(ITERS):
        shifted = scores + col_potential[None, :]
        highest = jnp.max(shifted, axis=1)
        summed = jnp.sum(jnp.exp2(shifted - highest[:, None]), axis=1)
        row_potential = -math.log2(total_points) - merged_rows(highest + jnp.log2(summed))
        shifted = scores + row_potential[:, None]
        highest = jnp.max(shifted, axis=0)
        summed = jnp.sum(jnp.exp2(shifted - highest[None, :]), axis=0)
        col_potential = -math.log2(total_centroids) - merged_cols(highest + jnp.log2(summed))
    transport = jnp.exp2(scores + row_potential[:, None] + col_potential[None, :])
    partial = lax.dot_general(
        transport.astype(jnp.bfloat16),
        points,
        (((0,), (0,)), ((), ())),
        preferred_element_type=jnp.float32,
    )
    own_rows = (total_centroids * scattered(partial)).astype(jnp.bfloat16)
    gathered = collected(own_rows)
    as_float = gathered.astype(jnp.float32)
    squares = jnp.sum(as_float * as_float, axis=1)
    cross_terms = lax.dot_general(
        points, gathered, (((1,), (1,)), ((), ())), preferred_element_type=jnp.float32
    )
    numerator = jnp.sum(transport * (squares[None, :] - 2.0 * cross_terms), axis=1)
    row_mass = jnp.sum(transport, axis=1)
    both = jnp.stack([numerator, row_mass])
    one, two, three = [cen_shift(both, step) for step in (1, 2, 3)]
    total = (both + two) + (one + three)
    distances = total[0] / total[1] / width
    return (own_rows, distances)


def solution(mesh):
    in_specs = (P("pts", None), P("cen", None))
    out_specs = (P(("cen", "pts"), None), P("pts"))
    return jax.shard_map(
        on_device, mesh=mesh, in_specs=in_specs, out_specs=out_specs, check_vma=False
    )
```

```python
import math

import jax
import jax.numpy as jnp
from jax import lax
from jax.experimental import pallas as pl
from jax.experimental.pallas import tpu as pltpu
from jax.sharding import PartitionSpec as P

ITERS = 3


sharpness = 4.0
LOG2E = math.log2(math.e)
C = 2
LANES = 128
SUB = 8
GROUP = 128
F32 = jnp.float32
BF16 = jnp.bfloat16


def other_core(value):
    size = lax.axis_size("pts")
    return lax.ppermute(value, "pts", [(i, i ^ 1) for i in range(size)])


def chip_groups():
    size = lax.axis_size("pts")
    return [[chip * C + core for chip in range(size // C)] for core in range(C)]


def exchange(value):
    return lax.all_to_all(value, "pts", 0, 0, axis_index_groups=chip_groups())


def from_chips(value):
    chips = lax.axis_size("pts") // C
    return exchange(jnp.broadcast_to(value[None], (chips,) + value.shape))


def cen_shift(value, step):
    size = lax.axis_size("cen")
    return lax.ppermute(value, "cen", [(i, (i + step) % size) for i in range(size)])


def spread_cols(value):
    theirs = jnp.roll(other_core(value), value.shape[1] // 2, axis=1)
    top = jnp.maximum(value, theirs)
    value = top + jnp.log2(jnp.exp2(value - top) + jnp.exp2(theirs - top))
    return from_chips(value)


def on_lanes(row):
    return jnp.broadcast_to(row, (LANES, row.shape[1])).T


def lane_sums(values):
    top = values[0]
    for value in values[1:]:
        top = jnp.maximum(top, value)
    total = jnp.exp2(values[0] - top)
    for value in values[1:]:
        total = total + jnp.exp2(value - top)
    return top, total


def close(top, total):
    highest = jnp.max(top, axis=0, keepdims=True)
    return highest + jnp.log2(jnp.sum(total * jnp.exp2(top - highest), axis=0, keepdims=True))


def group_pairs(scores_ref, group, cols, top_ref, total_ref):
    first = group * GROUP
    at = [slice(first + SUB * j, first + SUB * (j + 1)) for j in range(GROUP // SUB)]
    out = slice(group * SUB, (group + 1) * SUB)

    def step(block, carry):
        here = pl.ds(pl.multiple_of(block * LANES, LANES), LANES)
        values = [scores_ref[a, here] for a in at]
        if cols is not None:
            values = [v + c for v, c in zip(values, cols)]
        top, total = lane_sums(values)
        top_ref[out, here] = top
        total_ref[out, here] = total
        return carry

    lax.fori_loop(0, scores_ref.shape[1] // LANES, step, 0, unroll=2)


def score_kernel(
    core_ref, points_ref, centroids_ref, scores_ref, row_ref, split_ref, top_ref, total_ref, *, each
):
    count = points_ref.shape[0]
    rows = centroids_ref.shape[0]
    core = core_ref[0]
    blocks = rows // each // C

    def order(j, carry):
        for part in range(C):
            side = core if part == 0 else 1 - core
            start = pl.multiple_of((j * C + side) * each, each)
            here = pl.multiple_of((part * blocks + j) * each, each)
            split_ref[pl.ds(here, each), :] = centroids_ref[pl.ds(start, each), :]
        return carry

    lax.fori_loop(0, blocks, order, 0)
    chunk = 256
    for first in range(0, count, chunk):
        here = slice(first, first + chunk)
        product = lax.dot_general(
            split_ref[...],
            points_ref[here, :],
            (((1,), (1,)), ((), ())),
            preferred_element_type=F32,
        )
        scores_ref[:, here] = (sharpness * LOG2E) * product
    for group in range(rows // GROUP):
        group_pairs(scores_ref, group, None, top_ref, total_ref)
    row_ref[...] = close(top_ref[...], total_ref[...])


def col_potential(values_ref, level):
    values = values_ref[:, 0, :]
    highest = jnp.max(values, axis=0, keepdims=True)
    total = jnp.sum(jnp.exp2(values - highest), axis=0, keepdims=True)
    return level - (highest + jnp.log2(total))


def row_kernel(scores_ref, values_ref, row_ref, cols_ref, top_ref, total_ref, *, level):
    cols_ref[...] = on_lanes(col_potential(values_ref, level))
    for group in range(scores_ref.shape[0] // GROUP):
        cols = [
            cols_ref[pl.ds(group * GROUP + SUB * j, SUB), :] for j in range(GROUP // SUB)
        ]
        group_pairs(scores_ref, group, cols, top_ref, total_ref)
    row_ref[...] = close(top_ref[...], total_ref[...])


def col_kernel(
    scores_ref, own_ref, one_ref, two_ref, three_ref, col_ref, row_ref, top_ref, total_ref, *, level
):
    own, one, two, three = own_ref[...], one_ref[...], two_ref[...], three_ref[...]
    highest = jnp.maximum(jnp.maximum(own, two), jnp.maximum(one, three))
    even = jnp.exp2(own - highest) + jnp.exp2(two - highest)
    odd = jnp.exp2(one - highest) + jnp.exp2(three - highest)
    row_ref[...] = level - (highest + jnp.log2(even + odd))

    rows, count = scores_ref.shape
    at = [slice(LANES * j, LANES * (j + 1)) for j in range(count // LANES)]
    points = [jnp.broadcast_to(row_ref[:, a], (SUB, LANES)) for a in at]

    def step(block, carry):
        here = pl.ds(pl.multiple_of(block * SUB, SUB), SUB)
        top, total = lane_sums([scores_ref[here, a] + p for a, p in zip(at, points)])
        top_ref[here, :] = top
        total_ref[here, :] = total
        return carry

    lax.fori_loop(0, rows // SUB, step, 0, unroll=2)
    col_ref[...] = close(top_ref[...].T, total_ref[...].T)


def plan_of(scores_ref, first, row_ref, cols_ref):
    here = slice(first, first + GROUP)
    shift = jnp.concatenate([cols_ref[here, :]] * (scores_ref.shape[1] // LANES), axis=1)
    return jnp.exp2((scores_ref[here, :] + row_ref[...]) + shift)


def sums_of(scores_ref, row_ref, cols_ref, points_ref, sums_ref, half):
    rows = sums_ref.shape[0]
    for first in range(0, rows, GROUP):
        plan = plan_of(scores_ref, half * rows + first, row_ref, cols_ref)
        sums_ref[first : first + GROUP, :] = lax.dot_general(
            plan.astype(BF16),
            points_ref[...],
            (((1,), (0,)), ((), ())),
            preferred_element_type=F32,
        ).astype(sums_ref.dtype)


def give_kernel(scores_ref, row_ref, values_ref, points_ref, sums_ref, cols_ref, *, level):
    cols_ref[...] = on_lanes(col_potential(values_ref, level))
    sums_of(scores_ref, row_ref, cols_ref, points_ref, sums_ref, 1)


def keep_kernel(scores_ref, row_ref, cols_ref, points_ref, sums_ref):
    sums_of(scores_ref, row_ref, cols_ref, points_ref, sums_ref, 0)


def distance_kernel(scores_ref, row_ref, cols_ref, points_ref, fresh_ref, both_ref, *, half):
    rows = fresh_ref.shape[0]
    count = points_ref.shape[0]
    numerator = jnp.zeros((SUB, count), F32)
    mass = jnp.zeros((SUB, count), F32)
    for first in range(0, rows, GROUP):
        fresh = fresh_ref[first : first + GROUP, :]
        wide = fresh.astype(F32)
        squares = jnp.sum(wide * wide, axis=1, keepdims=True)
        cross = lax.dot_general(
            fresh, points_ref[...], (((1,), (1,)), ((), ())), preferred_element_type=F32
        )
        plan = plan_of(scores_ref, half * rows + first, row_ref, cols_ref)
        term = plan * (squares - 2.0 * cross)
        numerator = numerator + jnp.sum(term.reshape(GROUP // SUB, SUB, count), axis=0)
        mass = mass + jnp.sum(plan.reshape(GROUP // SUB, SUB, count), axis=0)
    both_ref[0:1, :] = jnp.sum(numerator, axis=0, keepdims=True)
    both_ref[1:2, :] = jnp.sum(mass, axis=0, keepdims=True)


VMEM = pl.BlockSpec(memory_space=pltpu.VMEM)
SCALAR = pl.BlockSpec(memory_space=pltpu.SMEM)


def call(kernel, outs, scratch, args, name, limit=24):
    return pl.pallas_call(
        kernel,
        out_shape=[jax.ShapeDtypeStruct(shape, dtype) for shape, dtype in outs],
        in_specs=[SCALAR if arg.dtype == jnp.int32 else VMEM for arg in args],
        out_specs=[VMEM] * len(outs),
        scratch_shapes=[pltpu.VMEM(shape, dtype) for shape, dtype in scratch],
        compiler_params=pltpu.CompilerParams(vmem_limit_bytes=limit << 20),
        name=name,
    )(*args)


def on_device(points, centroids):
    chips = lax.axis_size("pts") // C
    core = lax.axis_index("pts") % C
    count, width = points.shape
    rows = centroids.shape[0]
    half = rows // C
    each = rows // (chips * C)
    total_centroids = rows * lax.axis_size("cen")
    row_level = -math.log2(count * chips * C)
    col_level = -math.log2(total_centroids)

    pairs = [((rows // GROUP * SUB, count), F32)] * 2
    strip = ((rows, LANES), F32)
    line = ((1, count), F32)
    sums = (half, width)

    scores, part = call(
        lambda *refs: score_kernel(*refs, each=each),
        [((rows, count), F32), line],
        [((rows, width), BF16)] + pairs,
        [core.astype(jnp.int32).reshape(1), points, centroids],
        "scores",
    )
    for iteration in range(ITERS):
        if iteration:
            (part,) = call(
                lambda *refs: row_kernel(*refs, level=col_level),
                [line],
                [strip] + pairs,
                [scores, values],
                "rows",
            )
        others = [cen_shift(part, step) for step in (1, 2, 3)]
        col, row = call(
            lambda *refs: col_kernel(*refs, level=row_level),
            [((1, rows), F32), line],
            [strip] * 2,
            [scores, part] + others,
            "cols",
        )
        values = spread_cols(col)

    give, cols = call(
        lambda *refs: give_kernel(*refs, level=col_level),
        [(sums, BF16), strip],
        [],
        [scores, row, values, points],
        "give",
    )
    theirs = other_core(give)
    (keep,) = call(keep_kernel, [(sums, F32)], [], [scores, row, cols, points], "keep")
    pieces = exchange((keep + theirs.astype(F32)).astype(BF16).reshape(chips, each, width))
    own_rows = (total_centroids * jnp.sum(pieces.astype(F32), axis=0)).astype(BF16)
    mine = from_chips(own_rows).reshape(half, width)
    other = other_core(mine)
    terms = [
        call(
            lambda *refs: distance_kernel(*refs, half=part),
            [((2, count), F32)],
            [],
            [scores, row, cols, points, fresh],
            "terms",
        )[0]
        for part, fresh in enumerate((mine, other))
    ]
    both = terms[0] + terms[1]
    one, two, three = [cen_shift(both, step) for step in (1, 2, 3)]
    total = (both + two) + (one + three)
    distances = total[0] / total[1] / width
    return (own_rows, distances)


def solution(mesh):
    in_specs = (P("pts", None), P("cen", None))
    out_specs = (P(("cen", "pts"), None), P("pts"))
    return jax.shard_map(
        on_device, mesh=mesh, in_specs=in_specs, out_specs=out_specs, check_vma=False
    )
```

```python
import math

import jax
import jax.numpy as jnp
from jax import lax
from jax.experimental import pallas as pl
from jax.experimental.pallas import tpu as pltpu
from jax.sharding import PartitionSpec as P

ITERS = 3


sharpness = 4.0
LOG2E = math.log2(math.e)
C = 2
LANES = 128
SUB = 8
GROUP = 128
F32 = jnp.float32
BF16 = jnp.bfloat16


def other_core(value):
    size = lax.axis_size("pts")
    return lax.ppermute(value, "pts", [(i, i ^ 1) for i in range(size)])


def chip_groups():
    size = lax.axis_size("pts")
    return [[chip * C + core for chip in range(size // C)] for core in range(C)]


def exchange(value):
    return lax.all_to_all(value, "pts", 0, 0, axis_index_groups=chip_groups())


def from_chips(value):
    chips = lax.axis_size("pts") // C
    return exchange(jnp.broadcast_to(value[None], (chips,) + value.shape))


def cen_shift(value, step):
    size = lax.axis_size("cen")
    return lax.ppermute(value, "cen", [(i, (i + step) % size) for i in range(size)])


def spread_cols(value):
    theirs = jnp.roll(other_core(value), value.shape[1] // 2, axis=1)
    top = jnp.maximum(value, theirs)
    value = top + jnp.log2(jnp.exp2(value - top) + jnp.exp2(theirs - top))
    return from_chips(value)


def on_lanes(row):
    return jnp.broadcast_to(row, (LANES, row.shape[1])).T


def tree(values, join):
    values = list(values)
    while len(values) > 1:
        values = [join(*values[j : j + 2]) if j + 1 < len(values) else values[j]
                  for j in range(0, len(values), 2)]
    return values[0]


def lane_sums(values):
    top = tree(values, jnp.maximum)
    return top, tree([jnp.exp2(value - top) for value in values], jnp.add)


def close(top, total):
    highest = jnp.max(top, axis=0, keepdims=True)
    return highest + jnp.log2(jnp.sum(total * jnp.exp2(top - highest), axis=0, keepdims=True))


def group_pairs(scores_ref, group, cols, top_ref, total_ref):
    first = group * GROUP
    at = [slice(first + SUB * j, first + SUB * (j + 1)) for j in range(GROUP // SUB)]
    out = slice(group * SUB, (group + 1) * SUB)

    def step(block, carry):
        here = pl.ds(pl.multiple_of(block * LANES, LANES), LANES)
        values = [scores_ref[a, here] for a in at]
        if cols is not None:
            values = [v + c for v, c in zip(values, cols)]
        top, total = lane_sums(values)
        top_ref[out, here] = top
        total_ref[out, here] = total
        return carry

    lax.fori_loop(0, scores_ref.shape[1] // LANES, step, 0, unroll=2)


def score_kernel(
    core_ref, points_ref, centroids_ref, scores_ref, row_ref, split_ref, top_ref, total_ref, *, each
):
    count = points_ref.shape[0]
    rows = centroids_ref.shape[0]
    core = core_ref[0]
    blocks = rows // each // C

    def order(j, carry):
        for part in range(C):
            side = core if part == 0 else 1 - core
            start = pl.multiple_of((j * C + side) * each, each)
            here = pl.multiple_of((part * blocks + j) * each, each)
            split_ref[pl.ds(here, each), :] = centroids_ref[pl.ds(start, each), :]
        return carry

    lax.fori_loop(0, blocks, order, 0)
    chunk = 256
    for first in range(0, count, chunk):
        here = slice(first, first + chunk)
        product = lax.dot_general(
            split_ref[...],
            points_ref[here, :],
            (((1,), (1,)), ((), ())),
            preferred_element_type=F32,
        )
        scores_ref[:, here] = (sharpness * LOG2E) * product
    for group in range(rows // GROUP):
        group_pairs(scores_ref, group, None, top_ref, total_ref)
    row_ref[...] = close(top_ref[...], total_ref[...])


def col_potential(values_ref, level):
    values = values_ref[:, 0, :]
    highest = jnp.max(values, axis=0, keepdims=True)
    total = jnp.sum(jnp.exp2(values - highest), axis=0, keepdims=True)
    return level - (highest + jnp.log2(total))


def row_kernel(scores_ref, values_ref, row_ref, cols_ref, top_ref, total_ref, *, level):
    cols_ref[...] = on_lanes(col_potential(values_ref, level))
    for group in range(scores_ref.shape[0] // GROUP):
        cols = [
            cols_ref[pl.ds(group * GROUP + SUB * j, SUB), :] for j in range(GROUP // SUB)
        ]
        group_pairs(scores_ref, group, cols, top_ref, total_ref)
    row_ref[...] = close(top_ref[...], total_ref[...])


def row_potential(own_ref, one_ref, two_ref, three_ref, level):
    own, one, two, three = own_ref[...], one_ref[...], two_ref[...], three_ref[...]
    highest = jnp.maximum(jnp.maximum(own, two), jnp.maximum(one, three))
    even = jnp.exp2(own - highest) + jnp.exp2(two - highest)
    odd = jnp.exp2(one - highest) + jnp.exp2(three - highest)
    return level - (highest + jnp.log2(even + odd))


def col_kernel(
    scores_ref, own_ref, one_ref, two_ref, three_ref, col_ref, row_ref, top_ref, total_ref, *, level
):
    row_ref[...] = row_potential(own_ref, one_ref, two_ref, three_ref, level)
    rows, count = scores_ref.shape
    at = [slice(LANES * j, LANES * (j + 1)) for j in range(count // LANES)]
    points = [jnp.broadcast_to(row_ref[:, a], (SUB, LANES)) for a in at]

    def step(block, carry):
        here = pl.ds(pl.multiple_of(block * SUB, SUB), SUB)
        top, total = lane_sums([scores_ref[here, a] + p for a, p in zip(at, points)])
        top_ref[here, :] = top
        total_ref[here, :] = total
        return carry

    lax.fori_loop(0, rows // SUB, step, 0, unroll=2)
    col_ref[...] = close(top_ref[...].T, total_ref[...].T)


def sums_of(scores_ref, row_ref, points_ref, sums_ref, half):
    rows = sums_ref.shape[0]
    width = points_ref.shape[1]
    for first in range(0, rows, GROUP):
        here = slice(first, first + GROUP)
        far = slice(half * rows + first, half * rows + first + GROUP)
        shifted = scores_ref[far, :] + row_ref[...]
        top = jnp.max(shifted, axis=1, keepdims=True)
        weights = jnp.exp2(shifted - top)
        total = jnp.sum(weights, axis=1, keepdims=True)
        sums_ref[here, :width] = lax.dot_general(
            weights.astype(BF16),
            points_ref[...],
            (((1,), (0,)), ((), ())),
            preferred_element_type=F32,
        )
        lane = lax.broadcasted_iota(jnp.int32, (GROUP, LANES), 1)
        sums_ref[here, width:] = jnp.where(lane < LANES // 2, top, total)


def give_kernel(
    scores_ref, own_ref, one_ref, two_ref, three_ref, points_ref, sums_ref, row_ref, *, level
):
    row_ref[...] = row_potential(own_ref, one_ref, two_ref, three_ref, level)
    sums_of(scores_ref, row_ref, points_ref, sums_ref, 1)


def keep_kernel(scores_ref, row_ref, points_ref, sums_ref):
    sums_of(scores_ref, row_ref, points_ref, sums_ref, 0)


def thirds(value):
    high = value.astype(BF16).astype(F32)
    rest = value - high
    middle = rest.astype(BF16).astype(F32)
    return [high, middle, rest - middle]


FIELD = 8
SPAN = LANES // 2


def info_tile(columns):
    lane = lax.broadcasted_iota(jnp.int32, (SUB, LANES), 1)
    tile = jnp.zeros((SUB, LANES), F32)
    for n, column in enumerate(columns):
        for m, part in enumerate(thirds(column)):
            spot = n * FIELD + m
            tile = jnp.where(lane == spot, part[:SUB], tile)
            tile = jnp.where(lane == SPAN + spot, part[SUB:], tile)
    return tile.astype(BF16)


def info_column(tiles, n):
    lane = lax.broadcasted_iota(jnp.int32, tiles.shape, 2)
    halves = []
    for base in (n * FIELD, SPAN + n * FIELD):
        mask = (lane >= base) & (lane < base + 3)
        halves.append(jnp.sum(jnp.where(mask, tiles, 0.0), axis=2, keepdims=True))
    return jnp.concatenate(halves, axis=1)


def join_kernel(mine_ref, theirs_ref, pieces_ref):
    width = mine_ref.shape[1] - LANES
    chips = pieces_ref.shape[0]
    each = mine_ref.shape[0] // chips
    for chip in range(chips):
        here = slice(chip * each, (chip + 1) * each)
        tops = [ref[here, width : width + 1] for ref in (mine_ref, theirs_ref)]
        totals = [ref[here, width + SPAN : width + SPAN + 1] for ref in (mine_ref, theirs_ref)]
        top = jnp.maximum(*tops)
        scales = [jnp.exp2(t - top) for t in tops]
        total = totals[0] * scales[0] + totals[1] * scales[1]
        for b in range(width // LANES):
            lanes = slice(b * LANES, (b + 1) * LANES)
            both = mine_ref[here, lanes] * scales[0] + theirs_ref[here, lanes] * scales[1]
            pieces_ref[chip, b * each : (b + 1) * each, :] = both.astype(BF16)
        pieces_ref[chip, width // LANES * each :, :] = info_tile([top, total])


def own_kernel(pieces_ref, own_ref, fresh_ref, *, level):
    chips = pieces_ref.shape[0]
    each, width = own_ref.shape
    blocks = width // LANES
    tiles = pieces_ref[:, blocks * each :, :].astype(F32)
    tops = info_column(tiles, 0)
    totals = info_column(tiles, 1)
    top = jnp.max(tops, axis=0)
    scales = jnp.exp2(tops - top[None])
    total = jnp.sum(totals * scales, axis=0)
    fresh = []
    for b in range(blocks):
        here = slice(b * each, (b + 1) * each)
        parts = [pieces_ref[chip, here, :].astype(F32) * scales[chip] for chip in range(chips)]
        fresh.append((tree(parts, jnp.add) / total).astype(BF16))
        own_ref[:, b * LANES : (b + 1) * LANES] = fresh[-1]
    info = info_tile([level - (top + jnp.log2(total))])
    for chip in range(chips):
        for b in range(blocks):
            fresh_ref[chip, b * each : (b + 1) * each, :] = fresh[b]
        fresh_ref[chip, blocks * each :, :] = info


def distance_kernel(scores_ref, row_ref, points_ref, fresh_ref, both_ref, *, half):
    chips = fresh_ref.shape[0]
    count, width = points_ref.shape
    blocks = width // LANES
    each = (fresh_ref.shape[1] - SUB) // blocks
    numerator = jnp.zeros((SUB, count), F32)
    mass = jnp.zeros((SUB, count), F32)
    step = GROUP // each
    for chip in range(0, chips, step):
        some = slice(chip, chip + step)
        fresh = jnp.concatenate(
            [
                fresh_ref[some, b * each : (b + 1) * each, :].reshape(GROUP, LANES)
                for b in range(blocks)
            ],
            axis=1,
        )
        col = info_column(fresh_ref[some, blocks * each :, :].astype(F32), 0).reshape(GROUP, 1)
        wide = fresh.astype(F32)
        squares = jnp.sum(wide * wide, axis=1, keepdims=True)
        cross = lax.dot_general(
            fresh, points_ref[...], (((1,), (1,)), ((), ())), preferred_element_type=F32
        )
        first = (half * chips + chip) * each
        plan = jnp.exp2((scores_ref[first : first + GROUP, :] + row_ref[...]) + col)
        term = plan * (squares - 2.0 * cross)
        numerator = numerator + jnp.sum(term.reshape(GROUP // SUB, SUB, count), axis=0)
        mass = mass + jnp.sum(plan.reshape(GROUP // SUB, SUB, count), axis=0)
    both_ref[0:1, :] = jnp.sum(numerator, axis=0, keepdims=True)
    both_ref[1:2, :] = jnp.sum(mass, axis=0, keepdims=True)


VMEM = pl.BlockSpec(memory_space=pltpu.VMEM)
SCALAR = pl.BlockSpec(memory_space=pltpu.SMEM)


def call(kernel, outs, scratch, args, name, limit=24):
    return pl.pallas_call(
        kernel,
        out_shape=[jax.ShapeDtypeStruct(shape, dtype) for shape, dtype in outs],
        in_specs=[SCALAR if arg.dtype == jnp.int32 else VMEM for arg in args],
        out_specs=[VMEM] * len(outs),
        scratch_shapes=[pltpu.VMEM(shape, dtype) for shape, dtype in scratch],
        compiler_params=pltpu.CompilerParams(vmem_limit_bytes=limit << 20),
        name=name,
    )(*args)


def on_device(points, centroids):
    chips = lax.axis_size("pts") // C
    core = lax.axis_index("pts") % C
    count, width = points.shape
    rows = centroids.shape[0]
    half = rows // C
    each = rows // (chips * C)
    total_centroids = rows * lax.axis_size("cen")
    row_level = -math.log2(count * chips * C)
    col_level = -math.log2(total_centroids)

    pairs = [((rows // GROUP * SUB, count), F32)] * 2
    strip = ((rows, LANES), F32)
    line = ((1, count), F32)

    scores, part = call(
        lambda *refs: score_kernel(*refs, each=each),
        [((rows, count), F32), line],
        [((rows, width), BF16)] + pairs,
        [core.astype(jnp.int32).reshape(1), points, centroids],
        "scores",
    )
    for iteration in range(ITERS):
        if iteration:
            (part,) = call(
                lambda *refs: row_kernel(*refs, level=col_level),
                [line],
                [strip] + pairs,
                [scores, values],
                "rows",
            )
        partial = [part] + [cen_shift(part, step) for step in (1, 2, 3)]
        if iteration < ITERS - 1:
            col, row = call(
                lambda *refs: col_kernel(*refs, level=row_level),
                [((1, rows), F32), line],
                [strip] * 2,
                [scores] + partial,
                "cols",
            )
            values = spread_cols(col)

    wide = ((half, width + LANES), F32)
    piece = ((chips, each * width // LANES + SUB, LANES), BF16)
    give, row = call(
        lambda *refs: give_kernel(*refs, level=row_level),
        [wide, line],
        [],
        [scores] + partial + [points],
        "give",
    )
    theirs = other_core(give)
    (keep,) = call(keep_kernel, [wide], [], [scores, row, points], "keep")
    (pieces,) = call(join_kernel, [piece], [], [keep, theirs], "join")
    own_rows, fresh = call(
        lambda *refs: own_kernel(*refs, level=col_level),
        [((each, width), BF16), piece],
        [],
        [exchange(pieces)],
        "own",
    )
    mine = exchange(fresh)
    terms = [
        call(
            lambda *refs: distance_kernel(*refs, half=part),
            [((2, count), F32)],
            [],
            [scores, row, points, new],
            "terms",
        )[0]
        for part, new in enumerate((mine, other_core(mine)))
    ]
    both = terms[0] + terms[1]
    one, two, three = [cen_shift(both, step) for step in (1, 2, 3)]
    total = (both + two) + (one + three)
    distances = total[0] / total[1] / width
    return (own_rows, distances)


def solution(mesh):
    in_specs = (P("pts", None), P("cen", None))
    out_specs = (P(("cen", "pts"), None), P("pts"))
    return jax.shard_map(
        on_device, mesh=mesh, in_specs=in_specs, out_specs=out_specs, check_vma=False
    )
```

```python
import math

import jax
import jax.numpy as jnp
from jax import lax
from jax.experimental import pallas as pl
from jax.experimental.pallas import tpu as pltpu
from jax.sharding import PartitionSpec as P

ITERS = 3


sharpness = 4.0
LOG2E = math.log2(math.e)
C = 2
LANES = 128
SUB = 8
GROUP = 128
UNROLL = 16
F32 = jnp.float32
BF16 = jnp.bfloat16


def other_core(value):
    size = lax.axis_size("pts")
    return lax.ppermute(value, "pts", [(i, i ^ 1) for i in range(size)])


def chip_groups():
    size = lax.axis_size("pts")
    return [[chip * C + core for chip in range(size // C)] for core in range(C)]


def exchange(value):
    return lax.all_to_all(value, "pts", 0, 0, axis_index_groups=chip_groups())


def from_chips(value):
    chips = lax.axis_size("pts") // C
    return exchange(jnp.broadcast_to(value[None], (chips,) + value.shape))


def cen_shift(value, step):
    size = lax.axis_size("cen")
    return lax.ppermute(value, "cen", [(i, (i + step) % size) for i in range(size)])


def spread_cols(value):
    theirs = jnp.roll(other_core(value), value.shape[1] // 2, axis=1)
    top = jnp.maximum(value, theirs)
    value = top + jnp.log2(jnp.exp2(value - top) + jnp.exp2(theirs - top))
    return from_chips(value)


def on_lanes(row):
    return jnp.broadcast_to(row, (LANES, row.shape[1])).T


def tree(values, join):
    values = list(values)
    while len(values) > 1:
        values = [join(*values[j : j + 2]) if j + 1 < len(values) else values[j]
                  for j in range(0, len(values), 2)]
    return values[0]


def lane_sums(values):
    top = tree(values, jnp.maximum)
    return top, tree([jnp.exp2(value - top) for value in values], jnp.add)


def close(top, total):
    highest = jnp.max(top, axis=0, keepdims=True)
    return highest + jnp.log2(jnp.sum(total * jnp.exp2(top - highest), axis=0, keepdims=True))


def group_pairs(scores_ref, group, cols, top_ref, total_ref):
    first = group * GROUP
    at = [slice(first + SUB * j, first + SUB * (j + 1)) for j in range(GROUP // SUB)]
    out = slice(group * SUB, (group + 1) * SUB)

    def step(block, carry):
        here = pl.ds(pl.multiple_of(block * LANES, LANES), LANES)
        top, total = lane_sums([scores_ref[a, here] + c[...] for a, c in zip(at, cols)])
        top_ref[out, here] = top
        total_ref[out, here] = total
        return carry

    lax.fori_loop(0, scores_ref.shape[1] // LANES, step, 0, unroll=UNROLL)


def score_kernel(
    core_ref, points_ref, centroids_ref, scores_ref, row_ref, turned_ref, split_ref, *, each
):
    count = points_ref.shape[0]
    rows = centroids_ref.shape[0]
    core = core_ref[0]
    blocks = rows // each // C

    def order(j, carry):
        for part in range(C):
            side = core if part == 0 else 1 - core
            start = pl.multiple_of((j * C + side) * each, each)
            here = pl.multiple_of((part * blocks + j) * each, each)
            split_ref[pl.ds(here, each), :] = centroids_ref[pl.ds(start, each), :]
        return carry

    lax.fori_loop(0, blocks, order, 0, unroll=4)
    chunk = 256
    for first in range(0, count, chunk):
        here = slice(first, first + chunk)
        turned = points_ref[here, :].T
        turned_ref[:, here] = turned
        product = lax.dot_general(
            split_ref[...], turned, (((1,), (0,)), ((), ())), preferred_element_type=F32
        )
        score = (sharpness * LOG2E) * product
        scores_ref[:, here] = score
        top = jnp.max(score, axis=0, keepdims=True)
        total = jnp.sum(jnp.exp2(score - top), axis=0, keepdims=True)
        row_ref[:, here] = top + jnp.log2(total)


def col_potential(values_ref, level):
    values = values_ref[:, 0, :]
    highest = jnp.max(values, axis=0, keepdims=True)
    total = jnp.sum(jnp.exp2(values - highest), axis=0, keepdims=True)
    return level - (highest + jnp.log2(total))


def row_kernel(scores_ref, values_ref, row_ref, cols_ref, top_ref, total_ref, *, level):
    cols_ref[...] = on_lanes(col_potential(values_ref, level))
    for group in range(scores_ref.shape[0] // GROUP):
        cols = [
            cols_ref.at[pl.ds(group * GROUP + SUB * j, SUB), :] for j in range(GROUP // SUB)
        ]
        group_pairs(scores_ref, group, cols, top_ref, total_ref)
    row_ref[...] = close(top_ref[...], total_ref[...])


def row_potential(own_ref, one_ref, two_ref, three_ref, level):
    own, one, two, three = own_ref[...], one_ref[...], two_ref[...], three_ref[...]
    highest = jnp.maximum(jnp.maximum(own, two), jnp.maximum(one, three))
    even = jnp.exp2(own - highest) + jnp.exp2(two - highest)
    odd = jnp.exp2(one - highest) + jnp.exp2(three - highest)
    return level - (highest + jnp.log2(even + odd))


def col_kernel(
    scores_ref, own_ref, one_ref, two_ref, three_ref, col_ref, row_ref, top_ref, total_ref, *, level
):
    row_ref[...] = row_potential(own_ref, one_ref, two_ref, three_ref, level)
    rows, count = scores_ref.shape
    at = [slice(LANES * j, LANES * (j + 1)) for j in range(count // LANES)]

    def step(block, carry):
        here = pl.ds(pl.multiple_of(block * SUB, SUB), SUB)
        top, total = lane_sums([scores_ref[here, a] + row_ref[:, a] for a in at])
        top_ref[here, :] = top
        total_ref[here, :] = total
        return carry

    lax.fori_loop(0, rows // SUB, step, 0, unroll=UNROLL)
    col_ref[...] = close(top_ref[...].T, total_ref[...].T)


def sums_of(scores_ref, row_ref, points_ref, sums_ref, half):
    rows = sums_ref.shape[0]
    width = points_ref.shape[1]
    for first in range(0, rows, GROUP):
        here = slice(first, first + GROUP)
        far = slice(half * rows + first, half * rows + first + GROUP)
        shifted = scores_ref[far, :] + row_ref[...]
        top = jnp.max(shifted, axis=1, keepdims=True)
        weights = jnp.exp2(shifted - top)
        total = jnp.sum(weights, axis=1, keepdims=True)
        sums_ref[here, :width] = lax.dot_general(
            weights.astype(BF16),
            points_ref[...],
            (((1,), (0,)), ((), ())),
            preferred_element_type=F32,
        )
        lane = lax.broadcasted_iota(jnp.int32, (GROUP, LANES), 1)
        sums_ref[here, width:] = jnp.where(lane < LANES // 2, top, total)


def give_kernel(
    scores_ref, own_ref, one_ref, two_ref, three_ref, points_ref, sums_ref, row_ref, *, level
):
    row_ref[...] = row_potential(own_ref, one_ref, two_ref, three_ref, level)
    sums_of(scores_ref, row_ref, points_ref, sums_ref, 1)


def keep_kernel(scores_ref, row_ref, points_ref, sums_ref):
    sums_of(scores_ref, row_ref, points_ref, sums_ref, 0)


def thirds(value):
    high = value.astype(BF16).astype(F32)
    rest = value - high
    middle = rest.astype(BF16).astype(F32)
    return [high, middle, rest - middle]


FIELD = 8
SPAN = LANES // 2


def info_tiles(columns):
    lane = lax.broadcasted_iota(jnp.int32, columns[0][:, :SUB].shape, 2)
    tiles = jnp.zeros(lane.shape, F32)
    for n, column in enumerate(columns):
        both = jnp.where(lane < SPAN, column[:, :SUB], column[:, SUB:])
        for m, part in enumerate(thirds(both)):
            tiles = jnp.where(lane % SPAN == n * FIELD + m, part, tiles)
    return tiles.astype(BF16)


def info_column(tiles, n):
    lane = lax.broadcasted_iota(jnp.int32, tiles.shape, 2)
    halves = []
    for base in (n * FIELD, SPAN + n * FIELD):
        mask = (lane >= base) & (lane < base + 3)
        halves.append(jnp.sum(jnp.where(mask, tiles, 0.0), axis=2, keepdims=True))
    return jnp.concatenate(halves, axis=1)


def join_kernel(mine_ref, theirs_ref, pieces_ref):
    width = mine_ref.shape[1] - LANES
    chips = pieces_ref.shape[0]
    each = mine_ref.shape[0] // chips
    lane = lax.broadcasted_iota(jnp.int32, (mine_ref.shape[0], LANES), 1)
    tops, totals = [], []
    for ref in (mine_ref, theirs_ref):
        straight = ref[:, width:]
        swapped = pltpu.roll(straight, SPAN, 1)
        tops.append(jnp.where(lane < SPAN, straight, swapped))
        totals.append(jnp.where(lane < SPAN, swapped, straight))
    top = jnp.maximum(*tops)
    scales = [jnp.exp2(t - top) for t in tops]
    total = totals[0] * scales[0] + totals[1] * scales[1]
    for b in range(width // LANES):
        lanes = slice(b * LANES, (b + 1) * LANES)
        both = mine_ref[:, lanes] * scales[0] + theirs_ref[:, lanes] * scales[1]
        here = slice(b * each, (b + 1) * each)
        pieces_ref[:, here, :] = both.astype(BF16).reshape(chips, each, LANES)
    shape = (chips, each, LANES)
    tiles = info_tiles([top.reshape(shape), total.reshape(shape)])
    pieces_ref[:, width // LANES * each :, :] = tiles


def own_kernel(pieces_ref, own_ref, fresh_ref, *, level):
    chips = pieces_ref.shape[0]
    each, width = own_ref.shape
    blocks = width // LANES
    tiles = pieces_ref[:, blocks * each :, :].astype(F32)
    tops = info_column(tiles, 0)
    totals = info_column(tiles, 1)
    top = jnp.max(tops, axis=0)
    scales = jnp.exp2(tops - top[None])
    total = jnp.sum(totals * scales, axis=0)
    fresh = []
    for b in range(blocks):
        here = slice(b * each, (b + 1) * each)
        parts = [pieces_ref[chip, here, :].astype(F32) * scales[chip] for chip in range(chips)]
        fresh.append((tree(parts, jnp.add) / total).astype(BF16))
        own_ref[:, b * LANES : (b + 1) * LANES] = fresh[-1]
    col = jnp.broadcast_to(level - (top + jnp.log2(total)), (each, LANES))
    info = info_tiles([col[None]])[0]
    for chip in range(chips):
        for b in range(blocks):
            fresh_ref[chip, b * each : (b + 1) * each, :] = fresh[b]
        fresh_ref[chip, blocks * each :, :] = info


def distance_kernel(scores_ref, row_ref, turned_ref, fresh_ref, both_ref, *, half):
    chips = fresh_ref.shape[0]
    width, count = turned_ref.shape
    blocks = width // LANES
    each = (fresh_ref.shape[1] - SUB) // blocks
    numerator = jnp.zeros((SUB, count), F32)
    mass = jnp.zeros((SUB, count), F32)
    step = GROUP // each
    for chip in range(0, chips, step):
        some = slice(chip, chip + step)
        fresh = jnp.concatenate(
            [
                fresh_ref[some, b * each : (b + 1) * each, :].reshape(GROUP, LANES)
                for b in range(blocks)
            ],
            axis=1,
        )
        col = info_column(fresh_ref[some, blocks * each :, :].astype(F32), 0).reshape(GROUP, 1)
        wide = fresh.astype(F32)
        squares = jnp.sum(wide * wide, axis=1, keepdims=True)
        cross = lax.dot_general(
            fresh, turned_ref[...], (((1,), (0,)), ((), ())), preferred_element_type=F32
        )
        first = (half * chips + chip) * each
        plan = jnp.exp2((scores_ref[first : first + GROUP, :] + row_ref[...]) + col)
        term = plan * (squares - 2.0 * cross)
        numerator = numerator + jnp.sum(term.reshape(GROUP // SUB, SUB, count), axis=0)
        mass = mass + jnp.sum(plan.reshape(GROUP // SUB, SUB, count), axis=0)
    both_ref[0:1, :] = jnp.sum(numerator, axis=0, keepdims=True)
    both_ref[1:2, :] = jnp.sum(mass, axis=0, keepdims=True)


VMEM = pl.BlockSpec(memory_space=pltpu.VMEM)
SCALAR = pl.BlockSpec(memory_space=pltpu.SMEM)


def call(kernel, outs, scratch, args, name, limit=24):
    return pl.pallas_call(
        kernel,
        out_shape=[jax.ShapeDtypeStruct(shape, dtype) for shape, dtype in outs],
        in_specs=[SCALAR if arg.dtype == jnp.int32 else VMEM for arg in args],
        out_specs=[VMEM] * len(outs),
        scratch_shapes=[pltpu.VMEM(shape, dtype) for shape, dtype in scratch],
        compiler_params=pltpu.CompilerParams(vmem_limit_bytes=limit << 20),
        name=name,
    )(*args)


def on_device(points, centroids):
    chips = lax.axis_size("pts") // C
    core = lax.axis_index("pts") % C
    count, width = points.shape
    rows = centroids.shape[0]
    half = rows // C
    each = rows // (chips * C)
    total_centroids = rows * lax.axis_size("cen")
    row_level = -math.log2(count * chips * C)
    col_level = -math.log2(total_centroids)

    pairs = [((rows // GROUP * SUB, count), F32)] * 2
    strip = ((rows, LANES), F32)
    line = ((1, count), F32)

    scores, part, turned = call(
        lambda *refs: score_kernel(*refs, each=each),
        [((rows, count), F32), line, ((width, count), BF16)],
        [((rows, width), BF16)],
        [core.astype(jnp.int32).reshape(1), points, centroids],
        "scores",
    )
    for iteration in range(ITERS):
        if iteration:
            (part,) = call(
                lambda *refs: row_kernel(*refs, level=col_level),
                [line],
                [strip] + pairs,
                [scores, values],
                "rows",
            )
        partial = [part] + [cen_shift(part, step) for step in (1, 2, 3)]
        if iteration < ITERS - 1:
            col, row = call(
                lambda *refs: col_kernel(*refs, level=row_level),
                [((1, rows), F32), line],
                [strip] * 2,
                [scores] + partial,
                "cols",
            )
            values = spread_cols(col)

    wide = ((half, width + LANES), F32)
    piece = ((chips, each * width // LANES + SUB, LANES), BF16)
    give, row = call(
        lambda *refs: give_kernel(*refs, level=row_level),
        [wide, line],
        [],
        [scores] + partial + [points],
        "give",
    )
    theirs = other_core(give)
    (keep,) = call(keep_kernel, [wide], [], [scores, row, points], "keep")
    (pieces,) = call(join_kernel, [piece], [], [keep, theirs], "join")
    own_rows, fresh = call(
        lambda *refs: own_kernel(*refs, level=col_level),
        [((each, width), BF16), piece],
        [],
        [exchange(pieces)],
        "own",
    )
    mine = exchange(fresh)
    terms = [
        call(
            lambda *refs: distance_kernel(*refs, half=part),
            [((2, count), F32)],
            [],
            [scores, row, turned, new],
            "terms",
        )[0]
        for part, new in enumerate((mine, other_core(mine)))
    ]
    both = terms[0] + terms[1]
    one, two, three = [cen_shift(both, step) for step in (1, 2, 3)]
    total = (both + two) + (one + three)
    distances = total[0] / total[1] / width
    return (own_rows, distances)


def solution(mesh):
    in_specs = (P("pts", None), P("cen", None))
    out_specs = (P(("cen", "pts"), None), P("pts"))
    return jax.shard_map(
        on_device, mesh=mesh, in_specs=in_specs, out_specs=out_specs, check_vma=False
    )
```

```python
import math

import jax
import jax.numpy as jnp
from jax import lax
from jax.experimental import pallas as pl
from jax.experimental.pallas import tpu as pltpu
from jax.sharding import PartitionSpec as P

ITERS = 3


sharpness = 4.0
LOG2E = math.log2(math.e)
X, C = 4, 2
PARITIES = 2
LANES = 128
SUB = 8
GROUP = 128
UNROLL = 16
F32 = jnp.float32
BF16 = jnp.bfloat16


def place(z, x, core):
    return (z * X + x) * C + core


def partner(value, mask):
    size = lax.axis_size("pts")
    return lax.ppermute(value, "pts", [(i, i ^ mask) for i in range(size)])


def other_core(value):
    return partner(value, 1)


def other_parity(value):
    return partner(value, C)


def exchange(value, parities):
    slabs = lax.axis_size("pts") // (X * C)
    step = PARITIES // parities
    groups = [
        [place(z, x, core) for x in range(parity, X, step) for z in range(slabs)]
        for parity in range(step)
        for core in range(C)
    ]
    return lax.all_to_all(value, "pts", 0, 0, axis_index_groups=groups)


def from_chips(value):
    chips = lax.axis_size("pts") // C
    return exchange(jnp.broadcast_to(value[None], (chips,) + value.shape), PARITIES)


def cen_shift(value, step):
    size = lax.axis_size("cen")
    return lax.ppermute(value, "cen", [(i, (i + step) % size) for i in range(size)])


def spread_cols(value):
    theirs = jnp.roll(other_core(value), value.shape[1] // 2, axis=1)
    top = jnp.maximum(value, theirs)
    value = top + jnp.log2(jnp.exp2(value - top) + jnp.exp2(theirs - top))
    return from_chips(value)


def on_lanes(row):
    return jnp.broadcast_to(row, (LANES, row.shape[1])).T


def tree(values, join):
    values = list(values)
    while len(values) > 1:
        values = [join(*values[j : j + 2]) if j + 1 < len(values) else values[j]
                  for j in range(0, len(values), 2)]
    return values[0]


def lane_sums(values):
    top = tree(values, jnp.maximum)
    return top, tree([jnp.exp2(value - top) for value in values], jnp.add)


def close(top, total):
    highest = jnp.max(top, axis=0, keepdims=True)
    return highest + jnp.log2(jnp.sum(total * jnp.exp2(top - highest), axis=0, keepdims=True))


def group_pairs(scores_ref, group, cols, top_ref, total_ref):
    first = group * GROUP
    at = [slice(first + SUB * j, first + SUB * (j + 1)) for j in range(GROUP // SUB)]
    out = slice(group * SUB, (group + 1) * SUB)

    def step(block, carry):
        here = pl.ds(pl.multiple_of(block * LANES, LANES), LANES)
        top, total = lane_sums([scores_ref[a, here] + c[...] for a, c in zip(at, cols)])
        top_ref[out, here] = top
        total_ref[out, here] = total
        return carry

    lax.fori_loop(0, scores_ref.shape[1] // LANES, step, 0, unroll=UNROLL)


def score_kernel(
    sides_ref, points_ref, centroids_ref, scores_ref, row_ref, turned_ref, split_ref, *, each
):
    count = points_ref.shape[0]
    rows = centroids_ref.shape[0]
    core, parity = sides_ref[0], sides_ref[1]
    slabs = rows // (each * X * C)

    def order(z, carry):
        for n in range(X * C):
            core_side, parity_side, pair = n // X, n // PARITIES % PARITIES, n % PARITIES
            to_core = core if core_side == 0 else 1 - core
            to_parity = parity if parity_side == 0 else 1 - parity
            start = place(z, pair * PARITIES + to_parity, to_core) * each
            here = pl.ds(pl.multiple_of((n * slabs + z) * each, each), each)
            split_ref[here, :] = centroids_ref[pl.ds(pl.multiple_of(start, each), each), :]
        return carry

    lax.fori_loop(0, slabs, order, 0, unroll=2)
    chunk = 256
    for first in range(0, count, chunk):
        here = slice(first, first + chunk)
        turned = points_ref[here, :].T
        turned_ref[:, here] = turned
        product = lax.dot_general(
            split_ref[...], turned, (((1,), (0,)), ((), ())), preferred_element_type=F32
        )
        score = (sharpness * LOG2E) * product
        scores_ref[:, here] = score
        top = jnp.max(score, axis=0, keepdims=True)
        total = jnp.sum(jnp.exp2(score - top), axis=0, keepdims=True)
        row_ref[:, here] = top + jnp.log2(total)


def col_potential(values_ref, level):
    values = values_ref[:, 0, :]
    highest = jnp.max(values, axis=0, keepdims=True)
    total = jnp.sum(jnp.exp2(values - highest), axis=0, keepdims=True)
    return level - (highest + jnp.log2(total))


def common_order(sides_ref, row):
    size = row.shape[1] // (C * PARITIES)
    quarters = [row[:, n * size : (n + 1) * size] for n in range(C * PARITIES)]
    swapped = jnp.concatenate([quarters[n ^ 1] for n in range(C * PARITIES)], axis=1)
    return jnp.where(sides_ref[1] == 0, row, swapped)


def row_kernel(
    sides_ref, scores_ref, values_ref, row_ref, cols_ref, top_ref, total_ref, *, level
):
    cols_ref[...] = on_lanes(common_order(sides_ref, col_potential(values_ref, level)))
    for group in range(scores_ref.shape[0] // GROUP):
        cols = [
            cols_ref.at[pl.ds(group * GROUP + SUB * j, SUB), :] for j in range(GROUP // SUB)
        ]
        group_pairs(scores_ref, group, cols, top_ref, total_ref)
    row_ref[...] = close(top_ref[...], total_ref[...])


def row_potential(own_ref, one_ref, two_ref, three_ref, level):
    own, one, two, three = own_ref[...], one_ref[...], two_ref[...], three_ref[...]
    highest = jnp.maximum(jnp.maximum(own, two), jnp.maximum(one, three))
    even = jnp.exp2(own - highest) + jnp.exp2(two - highest)
    odd = jnp.exp2(one - highest) + jnp.exp2(three - highest)
    return level - (highest + jnp.log2(even + odd))


def col_kernel(
    sides_ref, scores_ref, own_ref, one_ref, two_ref, three_ref, col_ref, row_ref, top_ref, total_ref, *, level
):
    row_ref[...] = row_potential(own_ref, one_ref, two_ref, three_ref, level)
    rows, count = scores_ref.shape
    at = [slice(LANES * j, LANES * (j + 1)) for j in range(count // LANES)]

    def step(block, carry):
        here = pl.ds(pl.multiple_of(block * SUB, SUB), SUB)
        top, total = lane_sums([scores_ref[here, a] + row_ref[:, a] for a in at])
        top_ref[here, :] = top
        total_ref[here, :] = total
        return carry

    lax.fori_loop(0, rows // SUB, step, 0, unroll=UNROLL)
    col = close(top_ref[...].T, total_ref[...].T)
    col_ref[...] = common_order(sides_ref, col)


def sums_of(scores_ref, row_ref, points_ref, sums_ref, part):
    rows = sums_ref.shape[0]
    width = points_ref.shape[1]
    for first in range(0, rows, GROUP):
        here = slice(first, first + GROUP)
        far = slice(part * rows + first, part * rows + first + GROUP)
        shifted = scores_ref[far, :] + row_ref[...]
        top = jnp.max(shifted, axis=1, keepdims=True)
        weights = jnp.exp2(shifted - top)
        total = jnp.sum(weights, axis=1, keepdims=True)
        sums_ref[here, :width] = lax.dot_general(
            weights.astype(BF16),
            points_ref[...],
            (((1,), (0,)), ((), ())),
            preferred_element_type=F32,
        )
        lane = lax.broadcasted_iota(jnp.int32, (GROUP, LANES), 1)
        sums_ref[here, width:] = jnp.where(lane < LANES // 2, top, total)


def first_sums_kernel(
    scores_ref, own_ref, one_ref, two_ref, three_ref, points_ref, sums_ref, row_ref, *, part, level
):
    row_ref[...] = row_potential(own_ref, one_ref, two_ref, three_ref, level)
    sums_of(scores_ref, row_ref, points_ref, sums_ref, part)


def sums_kernel(scores_ref, row_ref, points_ref, sums_ref, *, part):
    sums_of(scores_ref, row_ref, points_ref, sums_ref, part)


def thirds(value):
    high = value.astype(BF16).astype(F32)
    rest = value - high
    middle = rest.astype(BF16).astype(F32)
    return [high, middle, rest - middle]


FIELD = 8
SPAN = LANES // 2


def info_tiles(columns):
    lane = lax.broadcasted_iota(jnp.int32, columns[0][:, :SUB].shape, 2)
    tiles = jnp.zeros(lane.shape, F32)
    for n, column in enumerate(columns):
        both = jnp.where(lane < SPAN, column[:, :SUB], column[:, SUB:])
        for m, part in enumerate(thirds(both)):
            tiles = jnp.where(lane % SPAN == n * FIELD + m, part, tiles)
    return tiles.astype(BF16)


def info_column(tiles, n):
    lane = lax.broadcasted_iota(jnp.int32, tiles.shape, 2)
    halves = []
    for base in (n * FIELD, SPAN + n * FIELD):
        mask = (lane >= base) & (lane < base + 3)
        halves.append(jnp.sum(jnp.where(mask, tiles, 0.0), axis=2, keepdims=True))
    return jnp.concatenate(halves, axis=1)


def join_kernel(mine_ref, theirs_ref, *refs):
    *near_ref, pieces_ref = refs
    rows, width = mine_ref.shape
    width = width - LANES
    chips = pieces_ref.shape[0]
    each = rows // chips
    blocks = width // LANES
    lane = lax.broadcasted_iota(jnp.int32, (rows, LANES), 1)
    tops, totals = [], []
    for ref in (mine_ref, theirs_ref):
        straight = ref[:, width:]
        swapped = pltpu.roll(straight, SPAN, 1)
        tops.append(jnp.where(lane < SPAN, straight, swapped))
        totals.append(jnp.where(lane < SPAN, swapped, straight))
    for ref in near_ref:
        tiles = ref[:, blocks * each :, :].astype(F32)
        for n, columns in enumerate((tops, totals)):
            column = info_column(tiles, n).reshape(rows, 1)
            columns.append(jnp.broadcast_to(column, (rows, LANES)))
    top = tree(tops, jnp.maximum)
    scales = [jnp.exp2(t - top) for t in tops]
    total = tree([t * scale for t, scale in zip(totals, scales)], jnp.add)
    for b in range(blocks):
        lanes = slice(b * LANES, (b + 1) * LANES)
        here = slice(b * each, (b + 1) * each)
        parts = [mine_ref[:, lanes], theirs_ref[:, lanes]]
        parts += [ref[:, here, :].astype(F32).reshape(rows, LANES) for ref in near_ref]
        joined = tree([part * scale for part, scale in zip(parts, scales)], jnp.add)
        pieces_ref[:, here, :] = joined.astype(BF16).reshape(chips, each, LANES)
    shape = (chips, each, LANES)
    tiles = info_tiles([top.reshape(shape), total.reshape(shape)])
    pieces_ref[:, blocks * each :, :] = tiles


def own_kernel(pieces_ref, own_ref, fresh_ref, *, level):
    chips = pieces_ref.shape[0]
    each, width = own_ref.shape
    blocks = width // LANES
    tiles = pieces_ref[:, blocks * each :, :].astype(F32)
    tops = info_column(tiles, 0)
    totals = info_column(tiles, 1)
    top = jnp.max(tops, axis=0)
    scales = jnp.exp2(tops - top[None])
    total = jnp.sum(totals * scales, axis=0)
    fresh = []
    for b in range(blocks):
        here = slice(b * each, (b + 1) * each)
        parts = [pieces_ref[chip, here, :].astype(F32) * scales[chip] for chip in range(chips)]
        fresh.append((tree(parts, jnp.add) / total).astype(BF16))
        own_ref[:, b * LANES : (b + 1) * LANES] = fresh[-1]
    col = jnp.broadcast_to(level - (top + jnp.log2(total)), (each, LANES))
    info = info_tiles([col[None]])[0]
    for chip in range(chips):
        for b in range(blocks):
            fresh_ref[chip, b * each : (b + 1) * each, :] = fresh[b]
        fresh_ref[chip, blocks * each :, :] = info


def distance_kernel(scores_ref, row_ref, turned_ref, fresh_ref, both_ref, *, part):
    chips = fresh_ref.shape[0]
    width, count = turned_ref.shape
    blocks = width // LANES
    each = (fresh_ref.shape[1] - SUB) // blocks
    numerator = jnp.zeros((SUB, count), F32)
    mass = jnp.zeros((SUB, count), F32)
    step = GROUP // each
    for chip in range(0, chips, step):
        some = slice(chip, chip + step)
        fresh = jnp.concatenate(
            [
                fresh_ref[some, b * each : (b + 1) * each, :].reshape(GROUP, LANES)
                for b in range(blocks)
            ],
            axis=1,
        )
        col = info_column(fresh_ref[some, blocks * each :, :].astype(F32), 0).reshape(GROUP, 1)
        wide = fresh.astype(F32)
        squares = jnp.sum(wide * wide, axis=1, keepdims=True)
        cross = lax.dot_general(
            fresh, turned_ref[...], (((1,), (0,)), ((), ())), preferred_element_type=F32
        )
        first = (part * chips + chip) * each
        plan = jnp.exp2((scores_ref[first : first + GROUP, :] + row_ref[...]) + col)
        term = plan * (squares - 2.0 * cross)
        numerator = numerator + jnp.sum(term.reshape(GROUP // SUB, SUB, count), axis=0)
        mass = mass + jnp.sum(plan.reshape(GROUP // SUB, SUB, count), axis=0)
    both_ref[0:1, :] = jnp.sum(numerator, axis=0, keepdims=True)
    both_ref[1:2, :] = jnp.sum(mass, axis=0, keepdims=True)


VMEM = pl.BlockSpec(memory_space=pltpu.VMEM)
SCALAR = pl.BlockSpec(memory_space=pltpu.SMEM)


def call(kernel, outs, scratch, args, limit=24):
    return pl.pallas_call(
        kernel,
        out_shape=[jax.ShapeDtypeStruct(shape, dtype) for shape, dtype in outs],
        in_specs=[SCALAR if arg.dtype == jnp.int32 else VMEM for arg in args],
        out_specs=[VMEM] * len(outs),
        scratch_shapes=[pltpu.VMEM(shape, dtype) for shape, dtype in scratch],
        compiler_params=pltpu.CompilerParams(vmem_limit_bytes=limit << 20),
    )(*args)


def on_device(points, centroids):
    chips = lax.axis_size("pts") // C
    here = lax.axis_index("pts")
    sides = jnp.stack([here % C, here // C % PARITIES]).astype(jnp.int32)
    count, width = points.shape
    rows = centroids.shape[0]
    parts = C * PARITIES
    each = rows // (chips * C)
    row_level = -math.log2(count * chips * C)
    col_level = -math.log2(rows * lax.axis_size("cen"))

    pairs = [((rows // GROUP * SUB, count), F32)] * 2
    strip = ((rows, LANES), F32)
    line = ((1, count), F32)

    scores, partial, turned = call(
        lambda *refs: score_kernel(*refs, each=each),
        [((rows, count), F32), line, ((width, count), BF16)],
        [((rows, width), BF16)],
        [sides, points, centroids],
    )
    for iteration in range(ITERS):
        if iteration:
            (partial,) = call(
                lambda *refs: row_kernel(*refs, level=col_level),
                [line],
                [strip] + pairs,
                [sides, scores, values],
            )
        lines = [partial] + [cen_shift(partial, step) for step in (1, 2, 3)]
        if iteration < ITERS - 1:
            col, row = call(
                lambda *refs: col_kernel(*refs, level=row_level),
                [((1, rows), F32), line],
                [strip] * 2,
                [sides, scores] + lines,
            )
            values = spread_cols(col)

    wide = ((rows // parts, width + LANES), F32)
    piece = ((chips // PARITIES, each * width // LANES + SUB, LANES), BF16)

    def sums(part):
        return call(
            lambda *refs: sums_kernel(*refs, part=part), [wide], [], [scores, row, points]
        )[0]

    def join(*args):
        return call(join_kernel, [piece], [], list(args))[0]

    first, row = call(
        lambda *refs: first_sums_kernel(*refs, part=3, level=row_level),
        [wide, line],
        [],
        [scores] + lines + [points],
    )
    theirs = other_core(first)
    near = other_parity(join(sums(1), theirs))
    theirs = other_core(sums(2))
    pieces = exchange(join(sums(0), theirs, near), 1)
    own_rows, fresh = call(
        lambda *refs: own_kernel(*refs, level=col_level),
        [((each, width), BF16), piece],
        [],
        [pieces],
    )

    def terms(part, new):
        return call(
            lambda *refs: distance_kernel(*refs, part=part),
            [((2, count), F32)],
            [],
            [scores, row, turned, new],
        )[0]

    mine = exchange(fresh, 1)
    near = other_parity(mine)
    theirs = other_core(mine)
    both = terms(0, mine) + terms(2, theirs)
    theirs = other_core(near)
    both = both + (terms(1, near) + terms(3, theirs))
    one, two, three = [cen_shift(both, step) for step in (1, 2, 3)]
    total = (both + two) + (one + three)
    distances = total[0] / total[1] / width
    return (own_rows, distances)


def solution(mesh):
    in_specs = (P("pts", None), P("cen", None))
    out_specs = (P(("cen", "pts"), None), P("pts"))

    return jax.shard_map(
        on_device, mesh=mesh, in_specs=in_specs, out_specs=out_specs, check_vma=False
    )
```

```python
import math

import jax
import jax.numpy as jnp
from jax import lax
from jax.experimental import pallas as pl
from jax.experimental.pallas import tpu as pltpu
from jax.sharding import PartitionSpec as P

ITERS = 3


sharpness = 4.0
LOG2E = math.log2(math.e)
X, C = 4, 2
PARITIES = 2
LANES = 128
SUB = 8
GROUP = 128
UNROLL = 16
F32 = jnp.float32
BF16 = jnp.bfloat16


def place(z, x, core):
    return (z * X + x) * C + core


def partner(value, mask):
    size = lax.axis_size("pts")
    return lax.ppermute(value, "pts", [(i, i ^ mask) for i in range(size)])


def other_core(value):
    return partner(value, 1)


def other_parity(value):
    return partner(value, C)


def exchange(value, parities):
    slabs = lax.axis_size("pts") // (X * C)
    step = PARITIES // parities
    groups = [
        [place(z, x, core) for z in range(slabs) for x in range(parity, X, step)]
        for parity in range(step)
        for core in range(C)
    ]
    return lax.all_to_all(value, "pts", 0, 0, axis_index_groups=groups)


def from_chips(value):
    chips = lax.axis_size("pts") // C
    return exchange(jnp.broadcast_to(value[None], (chips,) + value.shape), PARITIES)


def cen_shift(value, step):
    size = lax.axis_size("cen")
    return lax.ppermute(value, "cen", [(i, (i + step) % size) for i in range(size)])


def spread_cols(value):
    theirs = jnp.roll(other_core(value), value.shape[1] // 2, axis=1)
    top = jnp.maximum(value, theirs)
    value = top + jnp.log2(jnp.exp2(value - top) + jnp.exp2(theirs - top))
    return from_chips(value)


def on_lanes(row):
    return jnp.broadcast_to(row, (LANES, row.shape[1])).T


def tree(values, join):
    values = list(values)
    while len(values) > 1:
        values = [join(*values[j : j + 2]) if j + 1 < len(values) else values[j]
                  for j in range(0, len(values), 2)]
    return values[0]


def lane_sums(values):
    top = tree(values, jnp.maximum)
    return top, tree([jnp.exp2(value - top) for value in values], jnp.add)


def close(top, total):
    highest = jnp.max(top, axis=0, keepdims=True)
    return highest + jnp.log2(jnp.sum(total * jnp.exp2(top - highest), axis=0, keepdims=True))


def group_pairs(scores_ref, group, cols, top_ref, total_ref):
    first = group * GROUP
    at = [slice(first + SUB * j, first + SUB * (j + 1)) for j in range(GROUP // SUB)]
    out = slice(group * SUB, (group + 1) * SUB)

    def step(block, carry):
        here = pl.ds(pl.multiple_of(block * LANES, LANES), LANES)
        top, total = lane_sums([scores_ref[a, here] + c[...] for a, c in zip(at, cols)])
        top_ref[out, here] = top
        total_ref[out, here] = total
        return carry

    lax.fori_loop(0, scores_ref.shape[1] // LANES, step, 0, unroll=UNROLL)


def score_kernel(
    points_ref, centroids_ref, scores_ref, row_ref, turned_ref, split_ref, *, each
):
    count = points_ref.shape[0]
    rows = centroids_ref.shape[0]
    core = lax.axis_index("pts") % C
    parity = lax.axis_index("pts") // C % PARITIES
    slabs = rows // (each * X * C)

    def order(z, carry):
        for n in range(X * C):
            side, pair = n // (X // PARITIES), n % (X // PARITIES)
            to_core = core if side // PARITIES == 0 else 1 - core
            to_parity = parity if side % PARITIES == 0 else 1 - parity
            start = place(z, pair * PARITIES + to_parity, to_core) * each
            block = (side * slabs + z) * (X // PARITIES) + pair
            here = pl.ds(pl.multiple_of(block * each, each), each)
            split_ref[here, :] = centroids_ref[pl.ds(pl.multiple_of(start, each), each), :]
        return carry

    lax.fori_loop(0, slabs, order, 0, unroll=2)
    chunk = 256
    for first in range(0, count, chunk):
        here = slice(first, first + chunk)
        turned = points_ref[here, :].T
        turned_ref[:, here] = turned
        product = lax.dot_general(
            split_ref[...], turned, (((1,), (0,)), ((), ())), preferred_element_type=F32
        )
        score = (sharpness * LOG2E) * product
        scores_ref[:, here] = score
        top = jnp.max(score, axis=0, keepdims=True)
        total = jnp.sum(jnp.exp2(score - top), axis=0, keepdims=True)
        row_ref[:, here] = top + jnp.log2(total)


def col_potential(values_ref, level):
    values = values_ref[:, 0, :]
    highest = jnp.max(values, axis=0, keepdims=True)
    total = jnp.sum(jnp.exp2(values - highest), axis=0, keepdims=True)
    return level - (highest + jnp.log2(total))


def common_order(row):
    size = row.shape[1] // (C * PARITIES)
    quarters = [row[:, n * size : (n + 1) * size] for n in range(C * PARITIES)]
    swapped = jnp.concatenate([quarters[n ^ 1] for n in range(C * PARITIES)], axis=1)
    return jnp.where(lax.axis_index("pts") // C % PARITIES == 0, row, swapped)


def row_kernel(scores_ref, values_ref, row_ref, cols_ref, top_ref, total_ref, *, level):
    cols_ref[...] = on_lanes(common_order(col_potential(values_ref, level)))
    for group in range(scores_ref.shape[0] // GROUP):
        cols = [
            cols_ref.at[pl.ds(group * GROUP + SUB * j, SUB), :] for j in range(GROUP // SUB)
        ]
        group_pairs(scores_ref, group, cols, top_ref, total_ref)
    row_ref[...] = close(top_ref[...], total_ref[...])


def row_potential(own_ref, one_ref, two_ref, three_ref, level):
    own, one, two, three = own_ref[...], one_ref[...], two_ref[...], three_ref[...]
    highest = jnp.maximum(jnp.maximum(own, two), jnp.maximum(one, three))
    even = jnp.exp2(own - highest) + jnp.exp2(two - highest)
    odd = jnp.exp2(one - highest) + jnp.exp2(three - highest)
    return level - (highest + jnp.log2(even + odd))


def col_kernel(
    scores_ref, own_ref, one_ref, two_ref, three_ref, col_ref, row_ref, top_ref, total_ref, *, level
):
    row_ref[...] = row_potential(own_ref, one_ref, two_ref, three_ref, level)
    rows, count = scores_ref.shape
    at = [slice(LANES * j, LANES * (j + 1)) for j in range(count // LANES)]

    def step(block, carry):
        here = pl.ds(pl.multiple_of(block * SUB, SUB), SUB)
        top, total = lane_sums([scores_ref[here, a] + row_ref[:, a] for a in at])
        top_ref[here, :] = top
        total_ref[here, :] = total
        return carry

    lax.fori_loop(0, rows // SUB, step, 0, unroll=UNROLL)
    col = close(top_ref[...].T, total_ref[...].T)
    col_ref[...] = common_order(col)


def sums_of(scores_ref, row_ref, points_ref, sums_ref, part):
    rows = sums_ref.shape[0]
    width = points_ref.shape[1]
    for first in range(0, rows, GROUP):
        here = slice(first, first + GROUP)
        far = slice(part * rows + first, part * rows + first + GROUP)
        shifted = scores_ref[far, :] + row_ref[...]
        top = jnp.max(shifted, axis=1, keepdims=True)
        weights = jnp.exp2(shifted - top)
        total = jnp.sum(weights, axis=1, keepdims=True)
        sums_ref[here, :width] = lax.dot_general(
            weights.astype(BF16),
            points_ref[...],
            (((1,), (0,)), ((), ())),
            preferred_element_type=F32,
        )
        lane = lax.broadcasted_iota(jnp.int32, (GROUP, LANES), 1)
        sums_ref[here, width:] = jnp.where(lane < LANES // 2, top, total)


def first_sums_kernel(
    scores_ref, own_ref, one_ref, two_ref, three_ref, points_ref, sums_ref, row_ref, *, part, level
):
    row_ref[...] = row_potential(own_ref, one_ref, two_ref, three_ref, level)
    sums_of(scores_ref, row_ref, points_ref, sums_ref, part)


def sums_kernel(scores_ref, row_ref, points_ref, sums_ref, *, part):
    sums_of(scores_ref, row_ref, points_ref, sums_ref, part)


def thirds(value):
    high = value.astype(BF16).astype(F32)
    rest = value - high
    middle = rest.astype(BF16).astype(F32)
    return [high, middle, rest - middle]


FIELD = 8
SPAN = LANES // 2


def info_tiles(columns):
    lane = lax.broadcasted_iota(jnp.int32, columns[0][:, :SUB].shape, 2)
    tiles = jnp.zeros(lane.shape, F32)
    for n, column in enumerate(columns):
        both = jnp.where(lane < SPAN, column[:, :SUB], column[:, SUB:])
        for m, part in enumerate(thirds(both)):
            tiles = jnp.where(lane % SPAN == n * FIELD + m, part, tiles)
    return tiles.astype(BF16)


def info_column(tiles, n):
    lane = lax.broadcasted_iota(jnp.int32, tiles.shape, 2)
    halves = []
    for base in (n * FIELD, SPAN + n * FIELD):
        mask = (lane >= base) & (lane < base + 3)
        halves.append(jnp.sum(jnp.where(mask, tiles, 0.0), axis=2, keepdims=True))
    return jnp.concatenate(halves, axis=1)


def join_kernel(mine_ref, theirs_ref, *refs):
    *near_ref, pieces_ref = refs
    rows, width = mine_ref.shape
    width = width - LANES
    chips = pieces_ref.shape[0]
    each = rows // chips
    blocks = width // LANES
    lane = lax.broadcasted_iota(jnp.int32, (rows, LANES), 1)
    tops, totals = [], []
    for ref in (mine_ref, theirs_ref):
        straight = ref[:, width:]
        swapped = pltpu.roll(straight, SPAN, 1)
        tops.append(jnp.where(lane < SPAN, straight, swapped))
        totals.append(jnp.where(lane < SPAN, swapped, straight))
    for ref in near_ref:
        tiles = ref[:, blocks * each :, :].astype(F32)
        for n, columns in enumerate((tops, totals)):
            column = info_column(tiles, n).reshape(rows, 1)
            columns.append(jnp.broadcast_to(column, (rows, LANES)))
    top = tree(tops, jnp.maximum)
    scales = [jnp.exp2(t - top) for t in tops]
    total = tree([t * scale for t, scale in zip(totals, scales)], jnp.add)
    for b in range(blocks):
        lanes = slice(b * LANES, (b + 1) * LANES)
        here = slice(b * each, (b + 1) * each)
        parts = [mine_ref[:, lanes], theirs_ref[:, lanes]]
        parts += [ref[:, here, :].astype(F32).reshape(rows, LANES) for ref in near_ref]
        joined = tree([part * scale for part, scale in zip(parts, scales)], jnp.add)
        pieces_ref[:, here, :] = joined.astype(BF16).reshape(chips, each, LANES)
    shape = (chips, each, LANES)
    tiles = info_tiles([top.reshape(shape), total.reshape(shape)])
    pieces_ref[:, blocks * each :, :] = tiles


def own_kernel(pieces_ref, own_ref, fresh_ref, *, level):
    chips = pieces_ref.shape[0]
    each, width = own_ref.shape
    blocks = width // LANES
    tiles = pieces_ref[:, blocks * each :, :].astype(F32)
    tops = info_column(tiles, 0)
    totals = info_column(tiles, 1)
    top = jnp.max(tops, axis=0)
    scales = jnp.exp2(tops - top[None])
    total = jnp.sum(totals * scales, axis=0)
    fresh = []
    for b in range(blocks):
        here = slice(b * each, (b + 1) * each)
        parts = [pieces_ref[chip, here, :].astype(F32) * scales[chip] for chip in range(chips)]
        fresh.append((tree(parts, jnp.add) / total).astype(BF16))
        own_ref[:, b * LANES : (b + 1) * LANES] = fresh[-1]
    col = jnp.broadcast_to(level - (top + jnp.log2(total)), (each, LANES))
    info = info_tiles([col[None]])[0]
    for chip in range(chips):
        for b in range(blocks):
            fresh_ref[chip, b * each : (b + 1) * each, :] = fresh[b]
        fresh_ref[chip, blocks * each :, :] = info


def distance_kernel(scores_ref, row_ref, turned_ref, fresh_ref, both_ref, *, part):
    chips = fresh_ref.shape[0]
    width, count = turned_ref.shape
    blocks = width // LANES
    each = (fresh_ref.shape[1] - SUB) // blocks
    numerator = jnp.zeros((SUB, count), F32)
    mass = jnp.zeros((SUB, count), F32)
    step = GROUP // each
    for chip in range(0, chips, step):
        some = slice(chip, chip + step)
        fresh = jnp.concatenate(
            [
                fresh_ref[some, b * each : (b + 1) * each, :].reshape(GROUP, LANES)
                for b in range(blocks)
            ],
            axis=1,
        )
        col = info_column(fresh_ref[some, blocks * each :, :].astype(F32), 0).reshape(GROUP, 1)
        wide = fresh.astype(F32)
        squares = jnp.sum(wide * wide, axis=1, keepdims=True)
        cross = lax.dot_general(
            fresh, turned_ref[...], (((1,), (0,)), ((), ())), preferred_element_type=F32
        )
        first = (part * chips + chip) * each
        plan = jnp.exp2((scores_ref[first : first + GROUP, :] + row_ref[...]) + col)
        term = plan * (squares - 2.0 * cross)
        numerator = numerator + jnp.sum(term.reshape(GROUP // SUB, SUB, count), axis=0)
        mass = mass + jnp.sum(plan.reshape(GROUP // SUB, SUB, count), axis=0)
    both_ref[0:1, :] = jnp.sum(numerator, axis=0, keepdims=True)
    both_ref[1:2, :] = jnp.sum(mass, axis=0, keepdims=True)


VMEM = pl.BlockSpec(memory_space=pltpu.VMEM)


def call(kernel, outs, scratch, args, limit=24):
    return pl.pallas_call(
        kernel,
        out_shape=[jax.ShapeDtypeStruct(shape, dtype) for shape, dtype in outs],
        in_specs=[VMEM] * len(args),
        out_specs=[VMEM] * len(outs),
        scratch_shapes=[pltpu.VMEM(shape, dtype) for shape, dtype in scratch],
        compiler_params=pltpu.CompilerParams(vmem_limit_bytes=limit << 20),
    )(*args)


def on_device(points, centroids):
    chips = lax.axis_size("pts") // C
    count, width = points.shape
    rows = centroids.shape[0]
    parts = C * PARITIES
    each = rows // (chips * C)
    row_level = -math.log2(count * chips * C)
    col_level = -math.log2(rows * lax.axis_size("cen"))

    pairs = [((rows // GROUP * SUB, count), F32)] * 2
    strip = ((rows, LANES), F32)
    line = ((1, count), F32)

    scores, partial, turned = call(
        lambda *refs: score_kernel(*refs, each=each),
        [((rows, count), F32), line, ((width, count), BF16)],
        [((rows, width), BF16)],
        [points, centroids],
    )
    for iteration in range(ITERS):
        if iteration:
            (partial,) = call(
                lambda *refs: row_kernel(*refs, level=col_level),
                [line],
                [strip] + pairs,
                [scores, values],
            )
        lines = [partial] + [cen_shift(partial, step) for step in (1, 2, 3)]
        if iteration < ITERS - 1:
            col, row = call(
                lambda *refs: col_kernel(*refs, level=row_level),
                [((1, rows), F32), line],
                [strip] * 2,
                [scores] + lines,
            )
            values = spread_cols(col)

    wide = ((rows // parts, width + LANES), F32)
    piece = ((chips // PARITIES, each * width // LANES + SUB, LANES), BF16)

    def sums(part):
        return call(
            lambda *refs: sums_kernel(*refs, part=part), [wide], [], [scores, row, points]
        )[0]

    def join(*args):
        return call(join_kernel, [piece], [], list(args))[0]

    first, row = call(
        lambda *refs: first_sums_kernel(*refs, part=3, level=row_level),
        [wide, line],
        [],
        [scores] + lines + [points],
    )
    theirs = other_core(first)
    near = other_parity(join(sums(1), theirs))
    theirs = other_core(sums(2))
    pieces = exchange(join(sums(0), theirs, near), 1)
    own_rows, fresh = call(
        lambda *refs: own_kernel(*refs, level=col_level),
        [((each, width), BF16), piece],
        [],
        [pieces],
    )

    def terms(part, new):
        return call(
            lambda *refs: distance_kernel(*refs, part=part),
            [((2, count), F32)],
            [],
            [scores, row, turned, new],
        )[0]

    mine = exchange(fresh, 1)
    near = other_parity(mine)
    theirs = other_core(mine)
    both = terms(0, mine) + terms(2, theirs)
    theirs = other_core(near)
    both = both + (terms(1, near) + terms(3, theirs))
    one, two, three = [cen_shift(both, step) for step in (1, 2, 3)]
    total = (both + two) + (one + three)
    distances = total[0] / total[1] / width
    return (own_rows, distances)


def solution(mesh):
    in_specs = (P("pts", None), P("cen", None))
    out_specs = (P(("cen", "pts"), None), P("pts"))

    return jax.shard_map(
        on_device, mesh=mesh, in_specs=in_specs, out_specs=out_specs, check_vma=False
    )
```

```python
import math

import jax
import jax.numpy as jnp
from jax import lax
from jax.experimental import pallas as pl
from jax.experimental.pallas import tpu as pltpu
from jax.sharding import PartitionSpec as P

ITERS = 3


sharpness = 4.0
LOG2E = math.log2(math.e)
X, C = 4, 2
PARITIES = 2
LANES = 128
SUB = 8
GROUP = 128
UNROLL = 16
F32 = jnp.float32
BF16 = jnp.bfloat16


def place(z, x, core):
    return (z * X + x) * C + core


def partner(value, mask):
    size = lax.axis_size("pts")
    return lax.ppermute(value, "pts", [(i, i ^ mask) for i in range(size)])


def other_core(value):
    return partner(value, 1)


def parity_of(core):
    here = lax.axis_index("pts") // C
    return jnp.where(core == 0, here % PARITIES, here // X % PARITIES)


def other_parity(value):
    size = lax.axis_size("pts")
    flip = (C, C * X)
    return lax.ppermute(value, "pts", [(i, i ^ flip[i % C]) for i in range(size)])


def sorted_by_parity(chips):
    slabs = chips // X
    return [
        [
            [(z, x) for z in range(slabs) for x in range(X) if (z if core else x) % PARITIES == p]
            for p in range(PARITIES)
        ]
        for core in range(C)
    ]


def exchange(value, parities):
    chips = lax.axis_size("pts") // C
    if parities == PARITIES:
        groups = [[chip * C + core for chip in range(chips)] for core in range(C)]
    else:
        groups = [
            [place(z, x, core) for z, x in some]
            for core, parts in enumerate(sorted_by_parity(chips))
            for some in parts
        ]
    return lax.all_to_all(value, "pts", 0, 0, axis_index_groups=groups)


def from_chips(value):
    chips = lax.axis_size("pts") // C
    return exchange(jnp.broadcast_to(value[None], (chips,) + value.shape), PARITIES)


def cen_shift(value, step):
    size = lax.axis_size("cen")
    return lax.ppermute(value, "cen", [(i, (i + step) % size) for i in range(size)])


def spread_cols(value):
    theirs = jnp.roll(other_core(value), value.shape[1] // 2, axis=1)
    top = jnp.maximum(value, theirs)
    value = top + jnp.log2(jnp.exp2(value - top) + jnp.exp2(theirs - top))
    return from_chips(value)


def on_lanes(row):
    return jnp.broadcast_to(row, (LANES, row.shape[1])).T


def tree(values, join):
    values = list(values)
    while len(values) > 1:
        values = [join(*values[j : j + 2]) if j + 1 < len(values) else values[j]
                  for j in range(0, len(values), 2)]
    return values[0]


def lane_sums(values):
    top = tree(values, jnp.maximum)
    return top, tree([jnp.exp2(value - top) for value in values], jnp.add)


def close(top, total):
    highest = jnp.max(top, axis=0, keepdims=True)
    return highest + jnp.log2(jnp.sum(total * jnp.exp2(top - highest), axis=0, keepdims=True))


def group_pairs(scores_ref, group, cols, top_ref, total_ref):
    first = group * GROUP
    at = [slice(first + SUB * j, first + SUB * (j + 1)) for j in range(GROUP // SUB)]
    out = slice(group * SUB, (group + 1) * SUB)

    def step(block, carry):
        here = pl.ds(pl.multiple_of(block * LANES, LANES), LANES)
        top, total = lane_sums([scores_ref[a, here] + c[...] for a, c in zip(at, cols)])
        top_ref[out, here] = top
        total_ref[out, here] = total
        return carry

    lax.fori_loop(0, scores_ref.shape[1] // LANES, step, 0, unroll=UNROLL)


def score_kernel(
    points_ref, centroids_ref, scores_ref, row_ref, turned_ref, split_ref, *, each
):
    count = points_ref.shape[0]
    rows = centroids_ref.shape[0]
    core = lax.axis_index("pts") % C
    chips = rows // (each * C)

    def order(block, carry):
        for side in range(C * PARITIES):
            to_core = core if side // PARITIES == 0 else 1 - core
            parity = parity_of(to_core)
            parity = parity if side % PARITIES == 0 else 1 - parity
            along_x = place(block // PARITIES, block % PARITIES * PARITIES + parity, 0)
            along_z = place(block // X * PARITIES + parity, block % X, 1)
            start = jnp.where(to_core == 0, along_x, along_z) * each
            here = (side * (chips // PARITIES) + block) * each
            here = pl.ds(pl.multiple_of(here, each), each)
            split_ref[here, :] = centroids_ref[pl.ds(pl.multiple_of(start, each), each), :]
        return carry

    lax.fori_loop(0, chips // PARITIES, order, 0, unroll=2)
    chunk = 256
    for first in range(0, count, chunk):
        here = slice(first, first + chunk)
        turned = points_ref[here, :].T
        turned_ref[:, here] = turned
        product = lax.dot_general(
            split_ref[...], turned, (((1,), (0,)), ((), ())), preferred_element_type=F32
        )
        score = (sharpness * LOG2E) * product
        scores_ref[:, here] = score
        top = jnp.max(score, axis=0, keepdims=True)
        total = jnp.sum(jnp.exp2(score - top), axis=0, keepdims=True)
        row_ref[:, here] = top + jnp.log2(total)


def col_potential(values_ref, level):
    values = values_ref[:, 0, :]
    highest = jnp.max(values, axis=0, keepdims=True)
    total = jnp.sum(jnp.exp2(values - highest), axis=0, keepdims=True)
    return level - (highest + jnp.log2(total))


def common_order(row):
    core = lax.axis_index("pts") % C
    size = row.shape[1] // (C * PARITIES)
    quarters = [row[:, n * size : (n + 1) * size] for n in range(C * PARITIES)]
    out = []
    for half in range(C):
        straight = parity_of(core if half == 0 else 1 - core) == 0
        pair = quarters[half * PARITIES : (half + 1) * PARITIES]
        out += [jnp.where(straight, *pair), jnp.where(straight, *pair[::-1])]
    return jnp.concatenate(out, axis=1)


def row_kernel(scores_ref, values_ref, row_ref, cols_ref, top_ref, total_ref, *, level):
    cols_ref[...] = on_lanes(common_order(col_potential(values_ref, level)))
    for group in range(scores_ref.shape[0] // GROUP):
        cols = [
            cols_ref.at[pl.ds(group * GROUP + SUB * j, SUB), :] for j in range(GROUP // SUB)
        ]
        group_pairs(scores_ref, group, cols, top_ref, total_ref)
    row_ref[...] = close(top_ref[...], total_ref[...])


def row_potential(own_ref, one_ref, two_ref, three_ref, level):
    own, one, two, three = own_ref[...], one_ref[...], two_ref[...], three_ref[...]
    highest = jnp.maximum(jnp.maximum(own, two), jnp.maximum(one, three))
    even = jnp.exp2(own - highest) + jnp.exp2(two - highest)
    odd = jnp.exp2(one - highest) + jnp.exp2(three - highest)
    return level - (highest + jnp.log2(even + odd))


def col_kernel(
    scores_ref, own_ref, one_ref, two_ref, three_ref, col_ref, row_ref, top_ref, total_ref, *, level
):
    row_ref[...] = row_potential(own_ref, one_ref, two_ref, three_ref, level)
    rows, count = scores_ref.shape
    at = [slice(LANES * j, LANES * (j + 1)) for j in range(count // LANES)]

    def step(block, carry):
        here = pl.ds(pl.multiple_of(block * SUB, SUB), SUB)
        top, total = lane_sums([scores_ref[here, a] + row_ref[:, a] for a in at])
        top_ref[here, :] = top
        total_ref[here, :] = total
        return carry

    lax.fori_loop(0, rows // SUB, step, 0, unroll=UNROLL)
    col = close(top_ref[...].T, total_ref[...].T)
    col_ref[...] = common_order(col)


def sums_of(scores_ref, row_ref, points_ref, sums_ref, part):
    rows = sums_ref.shape[0]
    width = points_ref.shape[1]
    for first in range(0, rows, GROUP):
        here = slice(first, first + GROUP)
        far = slice(part * rows + first, part * rows + first + GROUP)
        shifted = scores_ref[far, :] + row_ref[...]
        top = jnp.max(shifted, axis=1, keepdims=True)
        weights = jnp.exp2(shifted - top)
        total = jnp.sum(weights, axis=1, keepdims=True)
        sums_ref[here, :width] = lax.dot_general(
            weights.astype(BF16),
            points_ref[...],
            (((1,), (0,)), ((), ())),
            preferred_element_type=F32,
        )
        lane = lax.broadcasted_iota(jnp.int32, (GROUP, LANES), 1)
        sums_ref[here, width:] = jnp.where(lane < LANES // 2, top, total)


def first_sums_kernel(
    scores_ref, own_ref, one_ref, two_ref, three_ref, points_ref, sums_ref, row_ref, *, part, level
):
    row_ref[...] = row_potential(own_ref, one_ref, two_ref, three_ref, level)
    sums_of(scores_ref, row_ref, points_ref, sums_ref, part)


def sums_kernel(scores_ref, row_ref, points_ref, sums_ref, *, part):
    sums_of(scores_ref, row_ref, points_ref, sums_ref, part)


def thirds(value):
    high = value.astype(BF16).astype(F32)
    rest = value - high
    middle = rest.astype(BF16).astype(F32)
    return [high, middle, rest - middle]


FIELD = 8
SPAN = LANES // 2


def info_tiles(columns):
    lane = lax.broadcasted_iota(jnp.int32, columns[0][:, :SUB].shape, 2)
    tiles = jnp.zeros(lane.shape, F32)
    for n, column in enumerate(columns):
        both = jnp.where(lane < SPAN, column[:, :SUB], column[:, SUB:])
        for m, part in enumerate(thirds(both)):
            tiles = jnp.where(lane % SPAN == n * FIELD + m, part, tiles)
    return tiles.astype(BF16)


def info_column(tiles, n):
    lane = lax.broadcasted_iota(jnp.int32, tiles.shape, 2)
    halves = []
    for base in (n * FIELD, SPAN + n * FIELD):
        mask = (lane >= base) & (lane < base + 3)
        halves.append(jnp.sum(jnp.where(mask, tiles, 0.0), axis=2, keepdims=True))
    return jnp.concatenate(halves, axis=1)


def join_kernel(mine_ref, theirs_ref, *refs):
    *near_ref, pieces_ref = refs
    rows, width = mine_ref.shape
    width = width - LANES
    chips = pieces_ref.shape[0]
    each = rows // chips
    blocks = width // LANES
    lane = lax.broadcasted_iota(jnp.int32, (rows, LANES), 1)
    tops, totals = [], []
    for ref in (mine_ref, theirs_ref):
        straight = ref[:, width:]
        swapped = pltpu.roll(straight, SPAN, 1)
        tops.append(jnp.where(lane < SPAN, straight, swapped))
        totals.append(jnp.where(lane < SPAN, swapped, straight))
    for ref in near_ref:
        tiles = ref[:, blocks * each :, :].astype(F32)
        for n, columns in enumerate((tops, totals)):
            column = info_column(tiles, n).reshape(rows, 1)
            columns.append(jnp.broadcast_to(column, (rows, LANES)))
    top = tree(tops, jnp.maximum)
    scales = [jnp.exp2(t - top) for t in tops]
    total = tree([t * scale for t, scale in zip(totals, scales)], jnp.add)
    for b in range(blocks):
        lanes = slice(b * LANES, (b + 1) * LANES)
        here = slice(b * each, (b + 1) * each)
        parts = [mine_ref[:, lanes], theirs_ref[:, lanes]]
        parts += [ref[:, here, :].astype(F32).reshape(rows, LANES) for ref in near_ref]
        joined = tree([part * scale for part, scale in zip(parts, scales)], jnp.add)
        pieces_ref[:, here, :] = joined.astype(BF16).reshape(chips, each, LANES)
    shape = (chips, each, LANES)
    tiles = info_tiles([top.reshape(shape), total.reshape(shape)])
    pieces_ref[:, blocks * each :, :] = tiles


def own_kernel(pieces_ref, own_ref, fresh_ref, *, level):
    chips = pieces_ref.shape[0]
    each, width = own_ref.shape
    blocks = width // LANES
    tiles = pieces_ref[:, blocks * each :, :].astype(F32)
    tops = info_column(tiles, 0)
    totals = info_column(tiles, 1)
    top = jnp.max(tops, axis=0)
    scales = jnp.exp2(tops - top[None])
    total = jnp.sum(totals * scales, axis=0)
    fresh = []
    for b in range(blocks):
        here = slice(b * each, (b + 1) * each)
        parts = [pieces_ref[chip, here, :].astype(F32) * scales[chip] for chip in range(chips)]
        fresh.append((tree(parts, jnp.add) / total).astype(BF16))
        own_ref[:, b * LANES : (b + 1) * LANES] = fresh[-1]
    col = jnp.broadcast_to(level - (top + jnp.log2(total)), (each, LANES))
    info = info_tiles([col[None]])[0]
    for chip in range(chips):
        for b in range(blocks):
            fresh_ref[chip, b * each : (b + 1) * each, :] = fresh[b]
        fresh_ref[chip, blocks * each :, :] = info


def distance_kernel(scores_ref, row_ref, turned_ref, fresh_ref, both_ref, *, part):
    chips = fresh_ref.shape[0]
    width, count = turned_ref.shape
    blocks = width // LANES
    each = (fresh_ref.shape[1] - SUB) // blocks
    numerator = jnp.zeros((SUB, count), F32)
    mass = jnp.zeros((SUB, count), F32)
    step = GROUP // each
    for chip in range(0, chips, step):
        some = slice(chip, chip + step)
        fresh = jnp.concatenate(
            [
                fresh_ref[some, b * each : (b + 1) * each, :].reshape(GROUP, LANES)
                for b in range(blocks)
            ],
            axis=1,
        )
        col = info_column(fresh_ref[some, blocks * each :, :].astype(F32), 0).reshape(GROUP, 1)
        wide = fresh.astype(F32)
        squares = jnp.sum(wide * wide, axis=1, keepdims=True)
        cross = lax.dot_general(
            fresh, turned_ref[...], (((1,), (0,)), ((), ())), preferred_element_type=F32
        )
        first = (part * chips + chip) * each
        plan = jnp.exp2((scores_ref[first : first + GROUP, :] + row_ref[...]) + col)
        term = plan * (squares - 2.0 * cross)
        numerator = numerator + jnp.sum(term.reshape(GROUP // SUB, SUB, count), axis=0)
        mass = mass + jnp.sum(plan.reshape(GROUP // SUB, SUB, count), axis=0)
    both_ref[0:1, :] = jnp.sum(numerator, axis=0, keepdims=True)
    both_ref[1:2, :] = jnp.sum(mass, axis=0, keepdims=True)


VMEM = pl.BlockSpec(memory_space=pltpu.VMEM)


def call(kernel, outs, scratch, args, limit=24):
    return pl.pallas_call(
        kernel,
        out_shape=[jax.ShapeDtypeStruct(shape, dtype) for shape, dtype in outs],
        in_specs=[VMEM] * len(args),
        out_specs=[VMEM] * len(outs),
        scratch_shapes=[pltpu.VMEM(shape, dtype) for shape, dtype in scratch],
        compiler_params=pltpu.CompilerParams(vmem_limit_bytes=limit << 20),
    )(*args)


def on_device(points, centroids):
    chips = lax.axis_size("pts") // C
    count, width = points.shape
    rows = centroids.shape[0]
    parts = C * PARITIES
    each = rows // (chips * C)
    row_level = -math.log2(count * chips * C)
    col_level = -math.log2(rows * lax.axis_size("cen"))

    pairs = [((rows // GROUP * SUB, count), F32)] * 2
    strip = ((rows, LANES), F32)
    line = ((1, count), F32)

    scores, partial, turned = call(
        lambda *refs: score_kernel(*refs, each=each),
        [((rows, count), F32), line, ((width, count), BF16)],
        [((rows, width), BF16)],
        [points, centroids],
    )
    for iteration in range(ITERS):
        if iteration:
            (partial,) = call(
                lambda *refs: row_kernel(*refs, level=col_level),
                [line],
                [strip] + pairs,
                [scores, values],
            )
        lines = [partial] + [cen_shift(partial, step) for step in (1, 2, 3)]
        if iteration < ITERS - 1:
            col, row = call(
                lambda *refs: col_kernel(*refs, level=row_level),
                [((1, rows), F32), line],
                [strip] * 2,
                [scores] + lines,
            )
            values = spread_cols(col)

    wide = ((rows // parts, width + LANES), F32)
    piece = ((chips // PARITIES, each * width // LANES + SUB, LANES), BF16)

    def sums(part):
        return call(
            lambda *refs: sums_kernel(*refs, part=part), [wide], [], [scores, row, points]
        )[0]

    def join(*args):
        return call(join_kernel, [piece], [], list(args))[0]

    first, row = call(
        lambda *refs: first_sums_kernel(*refs, part=3, level=row_level),
        [wide, line],
        [],
        [scores] + lines + [points],
    )
    theirs = other_core(first)
    near = other_parity(join(sums(1), theirs))
    theirs = other_core(sums(2))
    pieces = exchange(join(sums(0), theirs, near), 1)
    own_rows, fresh = call(
        lambda *refs: own_kernel(*refs, level=col_level),
        [((each, width), BF16), piece],
        [],
        [pieces],
    )

    def terms(part, new):
        return call(
            lambda *refs: distance_kernel(*refs, part=part),
            [((2, count), F32)],
            [],
            [scores, row, turned, new],
        )[0]

    mine = exchange(fresh, 1)
    near = other_parity(mine)
    theirs = other_core(mine)
    both = terms(0, mine) + terms(2, theirs)
    theirs = other_core(near)
    both = both + (terms(1, near) + terms(3, theirs))
    one, two, three = [cen_shift(both, step) for step in (1, 2, 3)]
    total = (both + two) + (one + three)
    distances = total[0] / total[1] / width
    return (own_rows, distances)


def solution(mesh):
    in_specs = (P("pts", None), P("cen", None))
    out_specs = (P(("cen", "pts"), None), P("pts"))

    return jax.shard_map(
        on_device, mesh=mesh, in_specs=in_specs, out_specs=out_specs, check_vma=False
    )
```

```python
import math

import jax
import jax.numpy as jnp
from jax import lax
from jax.experimental import pallas as pl
from jax.experimental.pallas import tpu as pltpu
from jax.sharding import PartitionSpec as P

ITERS = 3


sharpness = 4.0
LOG2E = math.log2(math.e)
X, C = 4, 2
PARITIES = 2
LANES = 128
SUB = 8
GROUP = 128
UNROLL = 16
F32 = jnp.float32
BF16 = jnp.bfloat16


def place(z, x, core):
    return (z * X + x) * C + core


def partner(value, mask):
    size = lax.axis_size("pts")
    return lax.ppermute(value, "pts", [(i, i ^ mask) for i in range(size)])


def other_core(value):
    return partner(value, 1)


def parity_of(core):
    here = lax.axis_index("pts") // C
    return jnp.where(core == 0, here % PARITIES, here // X % PARITIES)


def other_parity(value):
    size = lax.axis_size("pts")
    flip = (C, C * X)
    return lax.ppermute(value, "pts", [(i, i ^ flip[i % C]) for i in range(size)])


def sorted_by_parity(chips):
    slabs = chips // X
    return [
        [
            [(z, x) for z in range(slabs) for x in range(X) if (z if core else x) % PARITIES == p]
            for p in range(PARITIES)
        ]
        for core in range(C)
    ]


def exchange(value, parities):
    chips = lax.axis_size("pts") // C
    if parities == PARITIES:
        groups = [[chip * C + core for chip in range(chips)] for core in range(C)]
    else:
        groups = [
            [place(z, x, core) for z, x in some]
            for core, parts in enumerate(sorted_by_parity(chips))
            for some in parts
        ]
    return lax.all_to_all(value, "pts", 0, 0, axis_index_groups=groups)


def from_chips(value):
    chips = lax.axis_size("pts") // C
    return exchange(jnp.broadcast_to(value[None], (chips,) + value.shape), PARITIES)


def cen_shift(value, step):
    size = lax.axis_size("cen")
    return lax.ppermute(value, "cen", [(i, (i + step) % size) for i in range(size)])


def spread_cols(value):
    theirs = jnp.roll(other_core(value), value.shape[1] // 2, axis=1)
    top = jnp.maximum(value, theirs)
    value = top + jnp.log2(jnp.exp2(value - top) + jnp.exp2(theirs - top))
    return from_chips(value)


def cen_others(value):
    out = []
    for step in (1, 2, 3):
        out.append(cen_shift(value, step))
    return out


def on_lanes(row):
    return jnp.broadcast_to(row, (LANES, row.shape[1])).T


def tree(values, join):
    values = list(values)
    while len(values) > 1:
        values = [join(*values[j : j + 2]) if j + 1 < len(values) else values[j]
                  for j in range(0, len(values), 2)]
    return values[0]


def lane_sums(values):
    top = tree(values, jnp.maximum)
    return top, tree([jnp.exp2(value - top) for value in values], jnp.add)


def close(top, total):
    highest = jnp.max(top, axis=0, keepdims=True)
    return highest + jnp.log2(jnp.sum(total * jnp.exp2(top - highest), axis=0, keepdims=True))


def group_pairs(scores_ref, group, cols, top_ref, total_ref):
    first = group * GROUP
    at = [slice(first + SUB * j, first + SUB * (j + 1)) for j in range(GROUP // SUB)]
    out = slice(group * SUB, (group + 1) * SUB)

    def step(block, carry):
        here = pl.ds(pl.multiple_of(block * LANES, LANES), LANES)
        top, total = lane_sums([scores_ref[a, here] + c[...] for a, c in zip(at, cols)])
        top_ref[out, here] = top
        total_ref[out, here] = total
        return carry

    lax.fori_loop(0, scores_ref.shape[1] // LANES, step, 0, unroll=UNROLL)


def score_kernel(
    points_ref, centroids_ref, scores_ref, row_ref, turned_ref, split_ref, *, each
):
    count = points_ref.shape[0]
    rows = centroids_ref.shape[0]
    core = lax.axis_index("pts") % C
    chips = rows // (each * C)

    def order(block, carry):
        for side in range(C * PARITIES):
            to_core = core if side // PARITIES == 0 else 1 - core
            parity = parity_of(to_core)
            parity = parity if side % PARITIES == 0 else 1 - parity
            along_x = place(block // PARITIES, block % PARITIES * PARITIES + parity, 0)
            along_z = place(block // X * PARITIES + parity, block % X, 1)
            start = jnp.where(to_core == 0, along_x, along_z) * each
            here = (side * (chips // PARITIES) + block) * each
            here = pl.ds(pl.multiple_of(here, each), each)
            split_ref[here, :] = centroids_ref[pl.ds(pl.multiple_of(start, each), each), :]
        return carry

    lax.fori_loop(0, chips // PARITIES, order, 0, unroll=2)
    chunk = 256
    for first in range(0, count, chunk):
        here = slice(first, first + chunk)
        turned = points_ref[here, :].T
        turned_ref[:, here] = turned
        product = lax.dot_general(
            split_ref[...], turned, (((1,), (0,)), ((), ())), preferred_element_type=F32
        )
        score = (sharpness * LOG2E) * product
        scores_ref[:, here] = score
        top = jnp.max(score, axis=0, keepdims=True)
        total = jnp.sum(jnp.exp2(score - top), axis=0, keepdims=True)
        row_ref[:, here] = top + jnp.log2(total)


def col_potential(values_ref, level):
    values = values_ref[:, 0, :]
    highest = jnp.max(values, axis=0, keepdims=True)
    total = jnp.sum(jnp.exp2(values - highest), axis=0, keepdims=True)
    return level - (highest + jnp.log2(total))


def common_order(row):
    core = lax.axis_index("pts") % C
    size = row.shape[1] // (C * PARITIES)
    quarters = [row[:, n * size : (n + 1) * size] for n in range(C * PARITIES)]
    out = []
    for half in range(C):
        straight = parity_of(core if half == 0 else 1 - core) == 0
        pair = quarters[half * PARITIES : (half + 1) * PARITIES]
        out += [jnp.where(straight, *pair), jnp.where(straight, *pair[::-1])]
    return jnp.concatenate(out, axis=1)


def row_kernel(scores_ref, values_ref, row_ref, cols_ref, top_ref, total_ref, *, level):
    cols_ref[...] = on_lanes(common_order(col_potential(values_ref, level)))
    for group in range(scores_ref.shape[0] // GROUP):
        cols = [
            cols_ref.at[pl.ds(group * GROUP + SUB * j, SUB), :] for j in range(GROUP // SUB)
        ]
        group_pairs(scores_ref, group, cols, top_ref, total_ref)
    row_ref[...] = close(top_ref[...], total_ref[...])


def row_potential(own_ref, one_ref, two_ref, three_ref, level):
    own, one, two, three = own_ref[...], one_ref[...], two_ref[...], three_ref[...]
    highest = jnp.maximum(jnp.maximum(own, two), jnp.maximum(one, three))
    even = jnp.exp2(own - highest) + jnp.exp2(two - highest)
    odd = jnp.exp2(one - highest) + jnp.exp2(three - highest)
    return level - (highest + jnp.log2(even + odd))


def col_kernel(
    scores_ref, own_ref, one_ref, two_ref, three_ref, col_ref, row_ref, top_ref, total_ref, *, level
):
    row_ref[...] = row_potential(own_ref, one_ref, two_ref, three_ref, level)
    rows, count = scores_ref.shape
    at = [slice(LANES * j, LANES * (j + 1)) for j in range(count // LANES)]

    def step(block, carry):
        here = pl.ds(pl.multiple_of(block * SUB, SUB), SUB)
        top, total = lane_sums([scores_ref[here, a] + row_ref[:, a] for a in at])
        top_ref[here, :] = top
        total_ref[here, :] = total
        return carry

    lax.fori_loop(0, rows // SUB, step, 0, unroll=UNROLL)
    col = close(top_ref[...].T, total_ref[...].T)
    col_ref[...] = common_order(col)


def sums_of(scores_ref, row_ref, points_ref, sums_ref, part):
    rows = sums_ref.shape[0]
    width = points_ref.shape[1]
    for first in range(0, rows, GROUP):
        here = slice(first, first + GROUP)
        far = slice(part * rows + first, part * rows + first + GROUP)
        shifted = scores_ref[far, :] + row_ref[...]
        top = jnp.max(shifted, axis=1, keepdims=True)
        weights = jnp.exp2(shifted - top)
        total = jnp.sum(weights, axis=1, keepdims=True)
        sums_ref[here, :width] = lax.dot_general(
            weights.astype(BF16),
            points_ref[...],
            (((1,), (0,)), ((), ())),
            preferred_element_type=F32,
        )
        lane = lax.broadcasted_iota(jnp.int32, (GROUP, LANES), 1)
        sums_ref[here, width:] = jnp.where(lane < LANES // 2, top, total)


def first_sums_kernel(
    scores_ref, own_ref, one_ref, two_ref, three_ref, points_ref, sums_ref, row_ref, *, part, level
):
    row_ref[...] = row_potential(own_ref, one_ref, two_ref, three_ref, level)
    sums_of(scores_ref, row_ref, points_ref, sums_ref, part)


def sums_kernel(scores_ref, row_ref, points_ref, sums_ref, *, part):
    sums_of(scores_ref, row_ref, points_ref, sums_ref, part)


def thirds(value):
    high = value.astype(BF16).astype(F32)
    rest = value - high
    middle = rest.astype(BF16).astype(F32)
    return [high, middle, rest - middle]


FIELD = 8
SPAN = LANES // 2


def info_tiles(columns):
    lane = lax.broadcasted_iota(jnp.int32, columns[0][:, :SUB].shape, 2)
    tiles = jnp.zeros(lane.shape, F32)
    for n, column in enumerate(columns):
        both = jnp.where(lane < SPAN, column[:, :SUB], column[:, SUB:])
        for m, part in enumerate(thirds(both)):
            tiles = jnp.where(lane % SPAN == n * FIELD + m, part, tiles)
    return tiles.astype(BF16)


def info_column(tiles, n):
    lane = lax.broadcasted_iota(jnp.int32, tiles.shape, 2)
    halves = []
    for base in (n * FIELD, SPAN + n * FIELD):
        mask = (lane >= base) & (lane < base + 3)
        halves.append(jnp.sum(jnp.where(mask, tiles, 0.0), axis=2, keepdims=True))
    return jnp.concatenate(halves, axis=1)


def join_kernel(mine_ref, theirs_ref, *refs):
    *near_ref, pieces_ref = refs
    rows, width = mine_ref.shape
    width = width - LANES
    chips = pieces_ref.shape[0]
    each = rows // chips
    blocks = width // LANES
    lane = lax.broadcasted_iota(jnp.int32, (rows, LANES), 1)
    tops, totals = [], []
    for ref in (mine_ref, theirs_ref):
        straight = ref[:, width:]
        swapped = pltpu.roll(straight, SPAN, 1)
        tops.append(jnp.where(lane < SPAN, straight, swapped))
        totals.append(jnp.where(lane < SPAN, swapped, straight))
    for ref in near_ref:
        tiles = ref[:, blocks * each :, :].astype(F32)
        for n, columns in enumerate((tops, totals)):
            column = info_column(tiles, n).reshape(rows, 1)
            columns.append(jnp.broadcast_to(column, (rows, LANES)))
    top = tree(tops, jnp.maximum)
    scales = [jnp.exp2(t - top) for t in tops]
    total = tree([t * scale for t, scale in zip(totals, scales)], jnp.add)
    for b in range(blocks):
        lanes = slice(b * LANES, (b + 1) * LANES)
        here = slice(b * each, (b + 1) * each)
        parts = [mine_ref[:, lanes], theirs_ref[:, lanes]]
        parts += [ref[:, here, :].astype(F32).reshape(rows, LANES) for ref in near_ref]
        joined = tree([part * scale for part, scale in zip(parts, scales)], jnp.add)
        pieces_ref[:, here, :] = joined.astype(BF16).reshape(chips, each, LANES)
    shape = (chips, each, LANES)
    tiles = info_tiles([top.reshape(shape), total.reshape(shape)])
    pieces_ref[:, blocks * each :, :] = tiles


def own_kernel(pieces_ref, own_ref, fresh_ref, *, level):
    chips = pieces_ref.shape[0]
    each, width = own_ref.shape
    blocks = width // LANES
    tiles = pieces_ref[:, blocks * each :, :].astype(F32)
    tops = info_column(tiles, 0)
    totals = info_column(tiles, 1)
    top = jnp.max(tops, axis=0)
    scales = jnp.exp2(tops - top[None])
    total = jnp.sum(totals * scales, axis=0)
    fresh = []
    for b in range(blocks):
        here = slice(b * each, (b + 1) * each)
        parts = [pieces_ref[chip, here, :].astype(F32) * scales[chip] for chip in range(chips)]
        fresh.append((tree(parts, jnp.add) / total).astype(BF16))
        own_ref[:, b * LANES : (b + 1) * LANES] = fresh[-1]
    col = jnp.broadcast_to(level - (top + jnp.log2(total)), (each, LANES))
    info = info_tiles([col[None]])[0]
    for chip in range(chips):
        for b in range(blocks):
            fresh_ref[chip, b * each : (b + 1) * each, :] = fresh[b]
        fresh_ref[chip, blocks * each :, :] = info


def distance_kernel(scores_ref, row_ref, turned_ref, fresh_ref, both_ref, *, part):
    chips = fresh_ref.shape[0]
    width, count = turned_ref.shape
    blocks = width // LANES
    each = (fresh_ref.shape[1] - SUB) // blocks
    numerator = jnp.zeros((SUB, count), F32)
    mass = jnp.zeros((SUB, count), F32)
    step = GROUP // each
    for chip in range(0, chips, step):
        some = slice(chip, chip + step)
        fresh = jnp.concatenate(
            [
                fresh_ref[some, b * each : (b + 1) * each, :].reshape(GROUP, LANES)
                for b in range(blocks)
            ],
            axis=1,
        )
        col = info_column(fresh_ref[some, blocks * each :, :].astype(F32), 0).reshape(GROUP, 1)
        wide = fresh.astype(F32)
        squares = jnp.sum(wide * wide, axis=1, keepdims=True)
        cross = lax.dot_general(
            fresh, turned_ref[...], (((1,), (0,)), ((), ())), preferred_element_type=F32
        )
        first = (part * chips + chip) * each
        plan = jnp.exp2((scores_ref[first : first + GROUP, :] + row_ref[...]) + col)
        term = plan * (squares - 2.0 * cross)
        numerator = numerator + jnp.sum(term.reshape(GROUP // SUB, SUB, count), axis=0)
        mass = mass + jnp.sum(plan.reshape(GROUP // SUB, SUB, count), axis=0)
    both_ref[0:1, :] = jnp.sum(numerator, axis=0, keepdims=True)
    both_ref[1:2, :] = jnp.sum(mass, axis=0, keepdims=True)


def finish_kernel(own_ref, one_ref, two_ref, three_ref, distances_ref, *, width):
    total = (own_ref[...] + two_ref[...]) + (one_ref[...] + three_ref[...])
    distances_ref[...] = total[0:1] / total[1:2] / width


VMEM = pl.BlockSpec(memory_space=pltpu.VMEM)


def call(kernel, outs, scratch, args, limit=24):
    return pl.pallas_call(
        kernel,
        out_shape=[jax.ShapeDtypeStruct(shape, dtype) for shape, dtype in outs],
        in_specs=[VMEM] * len(args),
        out_specs=[VMEM] * len(outs),
        scratch_shapes=[pltpu.VMEM(shape, dtype) for shape, dtype in scratch],
        compiler_params=pltpu.CompilerParams(vmem_limit_bytes=limit << 20),
    )(*args)


def on_device(points, centroids):
    chips = lax.axis_size("pts") // C
    count, width = points.shape
    rows = centroids.shape[0]
    parts = C * PARITIES
    each = rows // (chips * C)
    row_level = -math.log2(count * chips * C)
    col_level = -math.log2(rows * lax.axis_size("cen"))

    pairs = [((rows // GROUP * SUB, count), F32)] * 2
    strip = ((rows, LANES), F32)
    line = ((1, count), F32)

    scores, partial, turned = call(
        lambda *refs: score_kernel(*refs, each=each),
        [((rows, count), F32), line, ((width, count), BF16)],
        [((rows, width), BF16)],
        [points, centroids],
    )
    for iteration in range(ITERS):
        if iteration:
            (partial,) = call(
                lambda *refs: row_kernel(*refs, level=col_level),
                [line],
                [strip] + pairs,
                [scores, values],
            )
        lines = [partial] + cen_others(partial)
        if iteration < ITERS - 1:
            col, row = call(
                lambda *refs: col_kernel(*refs, level=row_level),
                [((1, rows), F32), line],
                [strip] * 2,
                [scores] + lines,
            )
            values = spread_cols(col)

    wide = ((rows // parts, width + LANES), F32)
    piece = ((chips // PARITIES, each * width // LANES + SUB, LANES), BF16)

    def sums(part):
        return call(
            lambda *refs: sums_kernel(*refs, part=part), [wide], [], [scores, row, points]
        )[0]

    def join(*args):
        return call(join_kernel, [piece], [], list(args))[0]

    first, row = call(
        lambda *refs: first_sums_kernel(*refs, part=3, level=row_level),
        [wide, line],
        [],
        [scores] + lines + [points],
    )
    theirs = other_core(first)
    near = other_parity(join(sums(1), theirs))
    theirs = other_core(sums(2))
    pieces = exchange(join(sums(0), theirs, near), 1)
    own_rows, fresh = call(
        lambda *refs: own_kernel(*refs, level=col_level),
        [((each, width), BF16), piece],
        [],
        [pieces],
    )

    def terms(part, new):
        return call(
            lambda *refs: distance_kernel(*refs, part=part),
            [((2, count), F32)],
            [],
            [scores, row, turned, new],
        )[0]

    mine = exchange(fresh, 1)
    near = other_parity(mine)
    theirs = other_core(mine)
    both = terms(0, mine) + terms(2, theirs)
    theirs = other_core(near)
    both = both + (terms(1, near) + terms(3, theirs))
    (distances,) = call(
        lambda *refs: finish_kernel(*refs, width=width), [line], [], [both] + cen_others(both)
    )
    return (own_rows, distances.reshape(count))


def solution(mesh):
    in_specs = (P("pts", None), P("cen", None))
    out_specs = (P(("cen", "pts"), None), P("pts"))

    return jax.shard_map(
        on_device, mesh=mesh, in_specs=in_specs, out_specs=out_specs, check_vma=False
    )
```
